256 devices in a mesh: rows: 16 (over z_lo, x), tm: 16 (over y, z_hi, core).
Axes of the slice: x: 4, y: 4, z: 8 (z_hi: 2, z_lo: 4; z = z_hi * 4 + z_lo), core: 2. Of those that a mesh axis runs over, the one named last changes fastest.
Arguments:
- raw_signal: float32 [1024, 128, 128], P('tm', 'rows'), may hold values from -6 to 6
- fir_taps: float32 [61], replicated, may hold values from -0.75 to 0.75
- white_coef: float32 [25, 128, 128], P(None, 'rows'), may hold values from -1.25 to 1.25
- templates: bfloat16 [64, 61, 25], replicated, may hold values from -0.15625 to 0.15625
Outputs:
- whitened: bfloat16 [1024, 128, 128], P('tm', 'rows')
- best_score: float32 [1024, 128, 128], P('tm', 'rows')
The draws below stay inside these ranges and needn't reach their ends.
All inputs are finite; a program needn't handle non-finite values.
Results may differ from the reference program's by a relative error of at most 0.0049.
Values may be sent and summed in bfloat16 or wider, within the bound.
No kernel may reach another device: no remote copies, remote signals or barrier semaphores. Data moves between devices by JAX's collectives and lax.ppermute only.
A program may use at most 64 MiB of HBM per device.

```python
import jax
import jax.numpy as jnp
from jax import lax

COLS = 128
TEMPLATES = 64
TAPS = 61
TLEN = 61
TIME = 1024
GRID_ROWS = 128


def levels(stream_key, extent, shards, least, largest):
    def one(axis_at, blocks):
        draws = jax.random.uniform(jax.random.fold_in(jax.random.fold_in(stream_key, 6), axis_at), (blocks,), jnp.float32, least / len(shards), largest / len(shards))
        return jnp.repeat(jnp.exp(draws), extent[axis_at] // blocks).reshape((-1,) + (1,) * (len(extent) - axis_at - 1))

    factor_of = one(*shards[0])
    for cut in shards[1:]:
        factor_of = factor_of * one(*cut)
    return factor_of


def normal_values(own_key, extent, scale, limit, shards=(), held_as=jnp.bfloat16):
    factor_of = levels(own_key, extent, shards, -0.22, 0.18) if shards else 1.0
    result = jax.random.normal(own_key, extent, jnp.float32) * scale * factor_of
    return jnp.minimum(jnp.maximum(result, -limit), limit).astype(held_as)


def setup_inputs(seed: int = 0) -> dict:
    streams_of = jax.random.split(jax.random.key(seed), 5)
    raw_signal = normal_values(streams_of[0], (TIME, GRID_ROWS, COLS), 1.0, 6.0, ((0, 16), (1, 16)), jnp.float32)
    fir_taps = normal_values(streams_of[1], (TAPS,), TAPS ** -0.5, 0.75, (), jnp.float32)
    white_coef = normal_values(streams_of[2], (25, GRID_ROWS, COLS), 25 ** -0.5, 1.25, ((1, 16),), jnp.float32)
    templates = normal_values(streams_of[3], (TEMPLATES, TLEN, 25), (25 * TLEN) ** -0.5, 0.15625)
    return dict(raw_signal=raw_signal, fir_taps=fir_taps, white_coef=white_coef, templates=templates)


def template_bands(templates, block_len):
    by_spot = jnp.transpose(templates, (0, 2, 1))
    tmpl_len = templates.shape[1]
    shifted = [jnp.pad(by_spot, ((0, 0), (0, 0), (b, block_len - 1 - b))) for b in range(block_len)]
    stacked = jnp.stack(shifted, axis=1)
    return stacked.reshape(templates.shape[0] * block_len, 25 * (tmpl_len + block_len - 1))


def reference(raw_signal, fir_taps, white_coef, templates):
    num_steps, grid_rows, col_count = raw_signal.shape
    taps_back = fir_taps.shape[0] - 1
    padded = jnp.pad(raw_signal, ((taps_back, 0), (0, 0), (0, 0)))
    filt_sum = jnp.zeros(raw_signal.shape, jnp.float32)
    for k in range(taps_back + 1):
        filt_sum = filt_sum + fir_taps[k] * padded[taps_back - k:taps_back - k + num_steps]
    filtered = filt_sum.astype(jnp.bfloat16)
    filt_pad = jnp.pad(filtered.astype(jnp.float32), ((0, 0), (2, 2), (2, 2)))
    white_sum = jnp.zeros(raw_signal.shape, jnp.float32)
    for row_off in range(5):
        for col_off in range(5):
            white_sum = white_sum + white_coef[5 * row_off + col_off] * filt_pad[:, row_off:row_off + grid_rows, col_off:col_off + col_count]
    whitened = white_sum.astype(jnp.bfloat16)
    lag_len = templates.shape[1] - 1
    block_len = 8
    white_pad = jnp.pad(whitened.astype(jnp.float32), ((0, lag_len), (2, 2), (2, 2)))
    band_matrix = template_bands(templates.astype(jnp.float32), block_len)

    def score_block(i):
        window = lax.dynamic_slice_in_dim(white_pad, i * block_len, block_len + lag_len, 0)
        pieces = [window[:, row_off:row_off + grid_rows, col_off:col_off + col_count] for row_off in range(5) for col_off in range(5)]
        stacked = jnp.stack(pieces).reshape(25 * (block_len + lag_len), grid_rows * col_count)
        scores = jnp.dot(band_matrix, stacked, precision=lax.Precision.HIGHEST, preferred_element_type=jnp.float32)
        return jnp.max(scores.reshape(templates.shape[0], block_len, grid_rows * col_count), axis=0)

    best_rows = lax.map(score_block, jnp.arange(num_steps // block_len, dtype=jnp.int32))
    return whitened, best_rows.reshape(num_steps, grid_rows, col_count)
```

```python
import functools

import jax
import jax.numpy as jnp
from jax import lax
from jax.experimental import pallas as pl
from jax.experimental.pallas import tpu as pltpu
from jax.sharding import PartitionSpec as P

F32 = jnp.float32
BF16 = jnp.bfloat16
SHIFT = 4


def vmem():
    return pl.BlockSpec(memory_space=pltpu.VMEM)


def params():
    return pltpu.CompilerParams(vmem_limit_bytes=56 * 1024 * 1024)


def swap_pairs(array, axis, first):
    size = lax.axis_size(axis)
    pairs = []
    for low in range(first, size - 1, 2):
        pairs += [(low, low + 1), (low + 1, low)]
    return lax.ppermute(array, axis, pairs)


def step_by(array, axis, by):
    size = lax.axis_size(axis)
    return lax.ppermute(array, axis, [(i, i + by) for i in range(size) if 0 <= i + by < size])


def prep_kernel(line_ref, tmpl_ref, band_ref, lhs_ref, wide, mixed):
    spots, count, length = tmpl_ref.shape
    rows = band_ref.shape[0]
    line = jnp.broadcast_to(line_ref[...], (rows, 256))
    band = pltpu.roll(line, 0, 1, stride=1, stride_axis=0)
    high = band.astype(BF16)
    low = (band - high.astype(F32)).astype(BF16)
    band_ref[:, 0:256] = high
    band_ref[:, 256:512] = low
    band_ref[:, 512:768] = high

    wide[...] = jnp.zeros_like(wide)
    for s in range(spots):
        wide[s, :, 0:length] = tmpl_ref[s].astype(F32)
    for p in range((spots + 1) // 2):
        both = wide[2 * p]
        if 2 * p + 1 < spots:
            both = both + pltpu.roll(wide[2 * p + 1], 64, 1)
        for b in range(SHIFT):
            moved = pltpu.roll(both, b, 1) if b else both
            mixed[p, pl.ds(b, count, stride=SHIFT), :] = moved
        width = 128 if 2 * p + 1 < spots else 64
        lhs_ref[:, 128 * p : 128 * p + width] = mixed[p][:, :width].astype(BF16)


def prep(fir_taps, templates, span):
    count, length, spots = templates.shape
    taps = fir_taps.shape[0]
    line = jnp.pad(fir_taps[::-1], (span - taps + 1, 255 - span))[None]
    by_spot = jnp.transpose(templates, (2, 0, 1))
    return pl.pallas_call(
        prep_kernel,
        out_shape=(
            jax.ShapeDtypeStruct((2 * span, 768), BF16),
            jax.ShapeDtypeStruct((count * SHIFT, spots * 64), BF16),
        ),
        in_specs=[vmem()] * 2,
        out_specs=(vmem(), vmem()),
        scratch_shapes=[
            pltpu.VMEM((spots, count, 128), F32),
            pltpu.VMEM(((spots + 1) // 2, count * SHIFT, 128), F32),
        ],
        compiler_params=params(),
        cost_estimate=pl.CostEstimate(flops=10**7, bytes_accessed=2 * 10**6, transcendentals=0),
        name="prep",
    )(line, by_spot)


def fir_kernel(band_ref, raw_ref, near_ref, far_ref, coef_ref, filt_ref, up_ref, down_ref):
    rows, double, cols = filt_ref.shape
    span = double // 2
    even = lax.rem(lax.axis_index("tm"), 2) == 0
    columns = []
    for r in range(rows):
        near = near_ref[pl.ds(r, span, stride=rows), :]
        far = far_ref[pl.ds(r, span, stride=rows), :]
        own = raw_ref[pl.ds(r, span, stride=rows), :]
        before = jnp.where(even, far, near)
        after = jnp.where(even, near, far)
        line = jnp.concatenate([before, own, after, jnp.zeros_like(own)], axis=0)
        high = line.astype(BF16)
        low = (line - high.astype(F32)).astype(BF16)
        columns.append(jnp.concatenate([high, high, low], axis=0))
    for r in range(0, rows, 2):
        pair = jnp.concatenate(columns[r : r + 2], axis=1)
        out = jnp.dot(band_ref[...], pair, preferred_element_type=F32).astype(BF16)
        for k in range(2):
            piece = out[:, cols * k : cols * (k + 1)]
            filt_ref[r + k] = piece
            half = rows // 2
            side = up_ref if r + k < half else down_ref
            start = ((r + k) % half) * double
            side[start : start + double, :] = piece
    spots = coef_ref.shape[0] // rows
    base = rows // 2 * double
    for side, first in ((up_ref, 0), (down_ref, rows - 2)):
        side[base : base + 128, :] = jnp.zeros((128, cols), BF16)
        for k in range(2):
            coef = coef_ref[pl.ds(first + k, spots, stride=rows), :]
            high = coef.astype(BF16)
            low = (coef - high.astype(F32)).astype(BF16)
            side[base + 64 * k : base + 64 * k + spots, :] = high
            side[base + 64 * k + 32 : base + 64 * k + 32 + spots, :] = low


def fir(band, raw, near, far, coef, rows):
    span = raw.shape[0] // rows
    cols = raw.shape[1]
    message = jax.ShapeDtypeStruct((rows // 2 * 2 * span + 128, cols), BF16)
    return pl.pallas_call(
        fir_kernel,
        out_shape=(jax.ShapeDtypeStruct((rows, 2 * span, cols), BF16), message, message),
        in_specs=[vmem()] * 5,
        out_specs=(vmem(),) * 3,
        compiler_params=params(),
        cost_estimate=pl.CostEstimate(flops=2 * 10**8, bytes_accessed=2 * 10**6, transcendentals=0),
        name="fir",
    )(band, raw, near, far, coef)


def match_kernel(
    filt_ref, above_ref, below_ref, coef_ref, lhs_ref, white_ref, best_ref, moved, coefs, turn, slabs, natural, peaks
):
    rows, double, cols = filt_ref.shape
    span = double // 2
    half = rows // 2
    spots = coef_ref.shape[0] // rows
    wide = rows + 4
    lane = lax.broadcasted_iota(jnp.int32, (double, cols), 1)
    last = lax.axis_index("tm") == lax.axis_size("tm") - 1
    time = lax.broadcasted_iota(jnp.int32, (double, cols), 0)
    keep = jnp.logical_not(jnp.logical_and(last, time >= span))

    def shifted(x, b):
        if b == 2:
            return x
        out = pltpu.roll(x, (2 - b) % cols, 1)
        valid = lane >= 2 - b if b < 2 else lane < cols + 2 - b
        return jnp.where(valid, out, 0.0)

    def spread(x, row):
        x = x.astype(F32)
        for b in range(5):
            moved[b, row] = shifted(x, b)

    def from_above(k, _):
        spread(above_ref[pl.ds(pl.multiple_of(k * double, double), double), :], k)
        return 0

    def from_own(k, _):
        spread(filt_ref[k], half + k)
        return 0

    def from_below(k, _):
        spread(below_ref[pl.ds(pl.multiple_of(k * double, double), double), :], half + rows + k)
        return 0

    lax.fori_loop(0, half, from_above, 0)
    lax.fori_loop(0, rows, from_own, 0)
    lax.fori_loop(0, half, from_below, 0)

    base = half * double
    for k in range(2):
        for side, row in ((above_ref, k), (below_ref, rows + 2 + k)):
            high = side[base + 64 * k : base + 64 * k + 32, :].astype(F32)
            low = side[base + 64 * k + 32 : base + 64 * k + 64, :].astype(F32)
            coefs[row] = high + low
    for r in range(rows):
        coefs[2 + r, 0:spots] = coef_ref[pl.ds(r, spots, stride=rows), :]

    def whiten(r, _):
        total = jnp.zeros((double, cols), F32)
        for a in range(5):
            for b in range(5):
                s = 5 * a + b
                total = total + coefs[r, s : s + 1, :] * moved[b, r + half - 4 + a]
        total = jnp.where(keep, total, 0.0).astype(BF16).astype(F32)

        @pl.when(jnp.logical_and(r >= 2, r < rows + 2))
        def _():
            natural[pl.ds(r - 2, span, stride=rows), :] = total[:span]

        for b in range(5):
            turn[b, 0:double] = shifted(total, b)
            for f in range(4):
                slabs[f, b, r] = turn[b, SHIFT * f : SHIFT * f + double - 16, :].astype(BF16)
        return 0

    lax.fori_loop(0, wide, whiten, 0)
    white_ref[...] = natural[...].astype(BF16)

    def score(i, _):
        f = lax.rem(i, 4)
        start = pl.multiple_of(lax.div(i, 4) * 16, 16)
        for r in range(0, rows, 2):
            columns = [
                jnp.concatenate(
                    [slabs[f, b, r + k + a, pl.ds(start, 64), :] for a in range(5) for b in range(5)], axis=0
                )
                for k in range(2)
            ]
            window = jnp.concatenate(columns, axis=1)
            found = jnp.dot(lhs_ref[...], window, preferred_element_type=F32)
            top = jnp.max(found.reshape(found.shape[0] // 8, 8, 2 * cols), axis=0)
            top = jnp.maximum(top, pltpu.roll(top, 4, 0))
            peaks[i, r] = top[:, :cols]
            peaks[i, r + 1] = top[:, cols:]
        return 0

    steps = span // SHIFT
    lax.fori_loop(0, steps, score, 0)
    for i in range(steps):
        for r in range(rows):
            best_ref[pl.ds(SHIFT * rows * i + r, SHIFT, stride=rows), :] = peaks[i, r, 0:SHIFT, :]


def match(filt, above, below, coef, lhs):
    rows, double, cols = filt.shape
    span = double // 2
    return pl.pallas_call(
        match_kernel,
        out_shape=(
            jax.ShapeDtypeStruct((span * rows, cols), BF16),
            jax.ShapeDtypeStruct((span * rows, cols), F32),
        ),
        in_specs=[vmem()] * 5,
        out_specs=(vmem(), vmem()),
        scratch_shapes=[
            pltpu.VMEM((5, 2 * rows, double, cols), F32),
            pltpu.VMEM((rows + 4, 32, cols), F32),
            pltpu.VMEM((5, double, cols), F32),
            pltpu.VMEM((4, 5, rows + 4, double - 16, cols), BF16),
            pltpu.VMEM((span * rows, cols), F32),
            pltpu.VMEM((span // SHIFT, rows, 8, cols), F32),
        ],
        compiler_params=params(),
        cost_estimate=pl.CostEstimate(flops=14 * 10**9, bytes_accessed=2 * 10**6, transcendentals=0),
        name="match",
    )(filt, above, below, coef, lhs)


def shards(raw_signal, fir_taps, white_coef, templates):
    span, rows, cols = raw_signal.shape
    raw = raw_signal.reshape(span * rows, cols)
    coef = white_coef.reshape(-1, cols)
    far = swap_pairs(raw, "tm", 1)
    near = swap_pairs(raw, "tm", 0)
    band, lhs = prep(fir_taps, templates, span)
    filt, up, down = fir(band, raw, near, far, coef, rows)
    above = step_by(down, "rows", 1)
    below = step_by(up, "rows", -1)
    whitened, best = match(filt, above, below, coef, lhs)
    return whitened.reshape(span, rows, cols), best.reshape(span, rows, cols)


def solution(mesh):
    return jax.shard_map(
        shards,
        mesh=mesh,
        in_specs=(P("tm", "rows", None), P(), P(None, "rows", None), P()),
        out_specs=(P("tm", "rows", None), P("tm", "rows", None)),
        check_vma=False,
    )
```

```python
import jax
import jax.numpy as jnp
from jax import lax
from jax.experimental import pallas as pl
from jax.experimental.pallas import tpu as pltpu
from jax.sharding import PartitionSpec as P


F32 = jnp.float32
BF16 = jnp.bfloat16
SHIFT = 4


def vmem():
    return pl.BlockSpec(memory_space=pltpu.VMEM)


def params(mib):
    return pltpu.CompilerParams(vmem_limit_bytes=mib * 1024 * 1024)


def swap_pairs(array, axis, first):
    size = lax.axis_size(axis)
    pairs = []
    for low in range(first, size - 1, 2):
        pairs += [(low, low + 1), (low + 1, low)]
    return lax.ppermute(array, axis, pairs)


def step_by(array, axis, by):
    size = lax.axis_size(axis)
    return lax.ppermute(array, axis, [(i, i + by) for i in range(size) if 0 <= i + by < size])


def prep_kernel(line_ref, tmpl_ref, band_ref, lhs_ref, wide, mixed):
    spots, count, length = tmpl_ref.shape
    rows = band_ref.shape[0]
    line = jnp.broadcast_to(line_ref[...], (rows, 256))
    band = pltpu.roll(line, 0, 1, stride=1, stride_axis=0)
    high = band.astype(BF16)
    low = (band - high.astype(F32)).astype(BF16)
    band_ref[:, 0:256] = high
    band_ref[:, 256:512] = low
    band_ref[:, 512:768] = high

    wide[...] = jnp.zeros_like(wide)
    for s in range(spots):
        wide[s, :, 0:length] = tmpl_ref[s].astype(F32)
    for p in range((spots + 1) // 2):
        both = wide[2 * p]
        if 2 * p + 1 < spots:
            both = both + pltpu.roll(wide[2 * p + 1], 64, 1)
        for b in range(SHIFT):
            moved = pltpu.roll(both, b, 1) if b else both
            mixed[p, pl.ds(b, count, stride=SHIFT), :] = moved
        width = 128 if 2 * p + 1 < spots else 64
        lhs_ref[:, 128 * p : 128 * p + width] = mixed[p][:, :width].astype(BF16)


def prep(fir_taps, templates, span):
    count, _, spots = templates.shape
    taps = fir_taps.shape[0]
    line = jnp.pad(fir_taps[::-1], (span - taps + 1, 255 - span))[None]
    by_spot = jnp.transpose(templates, (2, 0, 1))
    return pl.pallas_call(
        prep_kernel,
        out_shape=(
            jax.ShapeDtypeStruct((2 * span, 768), BF16),
            jax.ShapeDtypeStruct((count * SHIFT, spots * 64), BF16),
        ),
        in_specs=[vmem()] * 2,
        out_specs=(vmem(), vmem()),
        scratch_shapes=[
            pltpu.VMEM((spots, count, 128), F32),
            pltpu.VMEM(((spots + 1) // 2, count * SHIFT, 128), F32),
        ],
        compiler_params=params(8),
        cost_estimate=pl.CostEstimate(flops=10**7, bytes_accessed=2 * 10**6, transcendentals=0),
        name="prep",
    )(line, by_spot)


def fir_kernel(band_ref, raw_ref, near_ref, far_ref, coef_ref, filt_ref, up_ref, down_ref, widened):
    rows, double, cols = filt_ref.shape
    span = double // 2
    even = lax.rem(lax.axis_index("tm"), 2) == 0
    widened[...] = far_ref[...].astype(F32)
    columns = []
    for r in range(rows):
        near = near_ref[pl.ds(r, span, stride=rows), :]
        far = widened[pl.ds(r, span, stride=rows), :]
        own = raw_ref[pl.ds(r, span, stride=rows), :]
        before = jnp.where(even, far, near)
        after = jnp.where(even, near, far)
        line = jnp.concatenate([before, own, after, jnp.zeros_like(own)], axis=0)
        high = line.astype(BF16)
        low = (line - high.astype(F32)).astype(BF16)
        columns.append(jnp.concatenate([high, high, low], axis=0))
    for r in range(0, rows, 2):
        pair = jnp.concatenate(columns[r : r + 2], axis=1)
        out = jnp.dot(band_ref[...], pair, preferred_element_type=F32).astype(BF16)
        for k in range(2):
            piece = out[:, cols * k : cols * (k + 1)]
            filt_ref[r + k] = piece
            half = rows // 2
            side = up_ref if r + k < half else down_ref
            start = ((r + k) % half) * double
            side[start : start + double, :] = piece
    spots = coef_ref.shape[0] // rows
    base = rows // 2 * double
    for side, first in ((up_ref, 0), (down_ref, rows - 2)):
        side[base : base + 128, :] = jnp.zeros((128, cols), BF16)
        for k in range(2):
            coef = coef_ref[pl.ds(first + k, spots, stride=rows), :]
            high = coef.astype(BF16)
            low = (coef - high.astype(F32)).astype(BF16)
            side[base + 64 * k : base + 64 * k + spots, :] = high
            side[base + 64 * k + 32 : base + 64 * k + 32 + spots, :] = low


def fir(band, raw, near, far, coef, rows):
    span = raw.shape[0] // rows
    cols = raw.shape[1]
    message = jax.ShapeDtypeStruct((rows // 2 * 2 * span + 128, cols), BF16)
    return pl.pallas_call(
        fir_kernel,
        out_shape=(jax.ShapeDtypeStruct((rows, 2 * span, cols), BF16), message, message),
        in_specs=[vmem()] * 5,
        out_specs=(vmem(),) * 3,
        scratch_shapes=[pltpu.VMEM(raw.shape, F32)],
        compiler_params=params(8),
        cost_estimate=pl.CostEstimate(flops=2 * 10**8, bytes_accessed=2 * 10**6, transcendentals=0),
        name="fir",
    )(band, raw, near, far, coef)


def match_kernel(
    filt_ref, above_ref, below_ref, coef_ref, lhs_ref, white_ref, best_ref, moved, coefs, turn, slabs, natural, peaks
):
    rows, double, cols = filt_ref.shape
    span = double // 2
    half = rows // 2
    spots = coef_ref.shape[0] // rows
    wide = rows + 4
    lane = lax.broadcasted_iota(jnp.int32, (double, cols), 1)
    last = lax.axis_index("tm") == lax.axis_size("tm") - 1
    time = lax.broadcasted_iota(jnp.int32, (double, cols), 0)
    keep = jnp.logical_not(jnp.logical_and(last, time >= span))

    def shifted(x, b):
        if b == 2:
            return x
        out = pltpu.roll(x, (2 - b) % cols, 1)
        valid = lane >= 2 - b if b < 2 else lane < cols + 2 - b
        return jnp.where(valid, out, 0.0)

    def spread(x, row):
        x = x.astype(F32)
        for b in range(5):
            moved[b, row] = shifted(x, b)

    def from_above(k, _):
        spread(above_ref[pl.ds(pl.multiple_of(k * double, double), double), :], k)
        return 0

    def from_own(k, _):
        spread(filt_ref[k], half + k)
        return 0

    def from_below(k, _):
        spread(below_ref[pl.ds(pl.multiple_of(k * double, double), double), :], half + rows + k)
        return 0

    lax.fori_loop(0, half, from_above, 0)
    lax.fori_loop(0, rows, from_own, 0)
    lax.fori_loop(0, half, from_below, 0)

    base = half * double
    for k in range(2):
        for side, row in ((above_ref, k), (below_ref, rows + 2 + k)):
            high = side[base + 64 * k : base + 64 * k + 32, :].astype(F32)
            low = side[base + 64 * k + 32 : base + 64 * k + 64, :].astype(F32)
            coefs[row] = high + low
    for r in range(rows):
        coefs[2 + r, 0:spots] = coef_ref[pl.ds(r, spots, stride=rows), :]

    def whiten(r, _):
        total = jnp.zeros((double, cols), F32)
        for a in range(5):
            for b in range(5):
                s = 5 * a + b
                total = total + coefs[r, s : s + 1, :] * moved[b, r + half - 4 + a]
        total = jnp.where(keep, total, 0.0).astype(BF16).astype(F32)

        @pl.when(jnp.logical_and(r >= 2, r < rows + 2))
        def _():
            natural[pl.ds(r - 2, span, stride=rows), :] = total[:span]

        for b in range(5):
            turn[b, 0:double] = shifted(total, b)
            for f in range(4):
                slabs[f, b, r] = turn[b, SHIFT * f : SHIFT * f + double - 16, :].astype(BF16)
        return 0

    lax.fori_loop(0, wide, whiten, 0)
    white_ref[...] = natural[...].astype(BF16)

    def score(i, _):
        f = lax.rem(i, 4)
        start = pl.multiple_of(lax.div(i, 4) * 16, 16)
        for r in range(0, rows, 2):
            columns = [
                jnp.concatenate(
                    [slabs[f, b, r + k + a, pl.ds(start, 64), :] for a in range(5) for b in range(5)], axis=0
                )
                for k in range(2)
            ]
            window = jnp.concatenate(columns, axis=1)
            found = jnp.dot(lhs_ref[...], window, preferred_element_type=F32)
            top = jnp.max(found.reshape(found.shape[0] // 8, 8, 2 * cols), axis=0)
            top = jnp.maximum(top, pltpu.roll(top, 4, 0))
            peaks[i, r] = top[:, :cols]
            peaks[i, r + 1] = top[:, cols:]
        return 0

    steps = span // SHIFT
    lax.fori_loop(0, steps, score, 0)
    for i in range(steps):
        for r in range(rows):
            best_ref[pl.ds(SHIFT * rows * i + r, SHIFT, stride=rows), :] = peaks[i, r, 0:SHIFT, :]


def match(filt, above, below, coef, lhs):
    rows, double, cols = filt.shape
    span = double // 2
    return pl.pallas_call(
        match_kernel,
        out_shape=(
            jax.ShapeDtypeStruct((span * rows, cols), BF16),
            jax.ShapeDtypeStruct((span * rows, cols), F32),
        ),
        in_specs=[vmem()] * 5,
        out_specs=(vmem(), vmem()),
        scratch_shapes=[
            pltpu.VMEM((5, 2 * rows, double, cols), F32),
            pltpu.VMEM((rows + 4, 32, cols), F32),
            pltpu.VMEM((5, double, cols), F32),
            pltpu.VMEM((4, 5, rows + 4, double - 16, cols), BF16),
            pltpu.VMEM((span * rows, cols), F32),
            pltpu.VMEM((span // SHIFT, rows, 8, cols), F32),
        ],
        compiler_params=params(20),
        cost_estimate=pl.CostEstimate(flops=14 * 10**9, bytes_accessed=2 * 10**6, transcendentals=0),
        name="match",
    )(filt, above, below, coef, lhs)


def shards(raw_signal, fir_taps, white_coef, templates):
    span, rows, cols = raw_signal.shape
    raw = raw_signal.reshape(span * rows, cols)
    coef = white_coef.reshape(-1, cols)
    far = swap_pairs(raw.astype(BF16), "tm", 1)
    near = swap_pairs(raw, "tm", 0)
    band, lhs = prep(fir_taps, templates, span)
    filt, up, down = fir(band, raw, near, far, coef, rows)
    above = step_by(down, "rows", 1)
    below = step_by(up, "rows", -1)
    whitened, best = match(filt, above, below, coef, lhs)
    return whitened.reshape(span, rows, cols), best.reshape(span, rows, cols)


def solution(mesh):
    return jax.shard_map(
        shards,
        mesh=mesh,
        in_specs=(P("tm", "rows", None), P(), P(None, "rows", None), P()),
        out_specs=(P("tm", "rows", None), P("tm", "rows", None)),
        check_vma=False,
    )
```

```python
import jax
import jax.numpy as jnp
from jax import lax
from jax.experimental import pallas as pl
from jax.experimental.pallas import tpu as pltpu
from jax.sharding import PartitionSpec as P


F32 = jnp.float32
BF16 = jnp.bfloat16
SHIFT = 4


def vmem():
    return pl.BlockSpec(memory_space=pltpu.VMEM)


def params(mib):
    return pltpu.CompilerParams(vmem_limit_bytes=mib * 1024 * 1024)


def swap_pairs(array, axis, first):
    size = lax.axis_size(axis)
    pairs = []
    for low in range(first, size - 1, 2):
        pairs += [(low, low + 1), (low + 1, low)]
    return lax.ppermute(array, axis, pairs)


def open_kernel(raw_ref, far_ref, keep_ref):
    skip = raw_ref.shape[0] - far_ref.shape[0]
    even = lax.rem(lax.axis_index("tm"), 2) == 0
    start = pl.multiple_of(jnp.where(even, 0, skip), 16)
    far_ref[...] = raw_ref[pl.ds(start, far_ref.shape[0]), :].astype(BF16)
    keep_ref[...] = raw_ref[...]


def opening(raw, rows, taps):
    return pl.pallas_call(
        open_kernel,
        out_shape=(
            jax.ShapeDtypeStruct(((taps - 1) * rows, raw.shape[1]), BF16),
            jax.ShapeDtypeStruct(raw.shape, F32),
        ),
        in_specs=[vmem()],
        out_specs=(vmem(), vmem()),
        compiler_params=params(4),
        cost_estimate=pl.CostEstimate(flops=10**5, bytes_accessed=10**6, transcendentals=0),
        name="opening",
    )(raw)


def prep_kernel(
    line_ref, tmpl_ref, coef_in_ref, band_ref, sum_ref, even_ref, odd_ref, coef_ref, wide, mixed
):
    coef_ref[...] = coef_in_ref[...]
    spots, count, length = tmpl_ref.shape
    rows = band_ref.shape[0]
    line = jnp.broadcast_to(line_ref[...], (rows, 256))
    band = pltpu.roll(line, 0, 1, stride=1, stride_axis=0)
    high = band.astype(BF16)
    low = (band - high.astype(F32)).astype(BF16)
    band_ref[:, 0:256] = high
    band_ref[:, 256:512] = low
    band_ref[:, 512:768] = high

    wide[...] = jnp.zeros_like(wide)
    for s in range(spots):
        wide[s, :, 0:length] = tmpl_ref[s].astype(F32)

    def even_spot(k):
        return wide[10 * (k // 5) + k % 5]

    def odd_spot(k):
        return wide[10 * (k // 5) + 5 + k % 5]

    def both_spots(k):
        return even_spot(k) + odd_spot(k) if k < 10 else even_spot(k)

    slot = 0
    for out_ref, piece, size in ((sum_ref, both_spots, 15), (even_ref, even_spot, 15), (odd_ref, odd_spot, 10)):
        for p in range(0, size, 2):
            pair = piece(p)
            if p + 1 < size:
                pair = pair + pltpu.roll(piece(p + 1), 64, 1)
            for b in range(SHIFT):
                moved = pltpu.roll(pair, b, 1) if b else pair
                mixed[slot, pl.ds(b, count, stride=SHIFT), :] = moved
            out_ref[:, 64 * p : 64 * p + 128] = mixed[slot].astype(BF16)
            slot += 1


def prep(fir_taps, templates, coef, span):
    count, _, spots = templates.shape
    taps = fir_taps.shape[0]
    line = jnp.pad(fir_taps[::-1], (span - taps + 1, 255 - span))[None]
    by_spot = jnp.transpose(templates, (2, 0, 1))
    return pl.pallas_call(
        prep_kernel,
        out_shape=(
            jax.ShapeDtypeStruct((2 * span, 768), BF16),
            jax.ShapeDtypeStruct((count * SHIFT, 16 * 64), BF16),
            jax.ShapeDtypeStruct((count * SHIFT, 16 * 64), BF16),
            jax.ShapeDtypeStruct((count * SHIFT, 10 * 64), BF16),
            jax.ShapeDtypeStruct(coef.shape, F32),
        ),
        in_specs=[vmem()] * 3,
        out_specs=(vmem(),) * 5,
        scratch_shapes=[
            pltpu.VMEM((spots, count, 128), F32),
            pltpu.VMEM((21, count * SHIFT, 128), F32),
        ],
        compiler_params=params(8),
        cost_estimate=pl.CostEstimate(flops=10**7, bytes_accessed=2 * 10**6, transcendentals=0),
        name="prep",
    )(line, by_spot, coef)


def fir_kernel(band_ref, raw_ref, near_ref, far_ref, coef_ref, filt_ref, first_ref, second_ref, widened):
    rows, double, cols = filt_ref.shape
    span = double // 2
    half = rows // 2
    even = lax.rem(lax.axis_index("tm"), 2) == 0
    short = far_ref.shape[0]
    skip = widened.shape[0] - short
    widened[0:skip, :] = jnp.zeros((skip, cols), F32)
    widened[short:, :] = jnp.zeros((skip, cols), F32)
    widened[pl.ds(pl.multiple_of(jnp.where(even, skip, 0), 16), short), :] = far_ref[...].astype(F32)
    columns = []
    for r in range(rows):
        near = near_ref[pl.ds(r, span, stride=rows), :]
        far = widened[pl.ds(r, span, stride=rows), :]
        own = raw_ref[pl.ds(r, span, stride=rows), :]
        before = jnp.where(even, far, near)
        after = jnp.where(even, near, far)
        line = jnp.concatenate([before, own, after, jnp.zeros_like(own)], axis=0)
        high = line.astype(BF16)
        low = (line - high.astype(F32)).astype(BF16)
        columns.append(jnp.concatenate([high, high, low], axis=0))
    for r in range(0, rows, 2):
        pair = jnp.concatenate(columns[r : r + 2], axis=1)
        out = jnp.dot(band_ref[...], pair, preferred_element_type=F32).astype(BF16)
        filt_ref[r] = out[:, :cols]
        filt_ref[r + 1] = out[:, cols:]
    spots = coef_ref.shape[0] // rows
    base = half * double
    upper = lax.rem(lax.axis_index("rows"), 2) == 0
    for side, at_end in ((first_ref, upper), (second_ref, jnp.logical_not(upper))):
        start = jnp.where(at_end, half, 0)
        for k in range(half):
            side[double * k : double * (k + 1), :] = filt_ref[start + k]
        side[base : base + 128, :] = jnp.zeros((128, cols), BF16)
        edge = jnp.where(at_end, rows - 2, 0)
        for k in range(2):
            coef = coef_ref[pl.ds(edge + k, spots, stride=rows), :]
            high = coef.astype(BF16)
            low = (coef - high.astype(F32)).astype(BF16)
            side[base + 64 * k : base + 64 * k + spots, :] = high
            side[base + 64 * k + 32 : base + 64 * k + 32 + spots, :] = low


def fir(band, raw, near, far, coef, rows):
    span = raw.shape[0] // rows
    cols = raw.shape[1]
    message = jax.ShapeDtypeStruct((rows // 2 * 2 * span + 128, cols), BF16)
    return pl.pallas_call(
        fir_kernel,
        out_shape=(jax.ShapeDtypeStruct((rows, 2 * span, cols), BF16), message, message),
        in_specs=[vmem()] * 5,
        out_specs=(vmem(),) * 3,
        scratch_shapes=[pltpu.VMEM(raw.shape, F32)],
        compiler_params=params(8),
        cost_estimate=pl.CostEstimate(flops=2 * 10**8, bytes_accessed=2 * 10**6, transcendentals=0),
        name="fir",
    )(band, raw, near, far, coef)


def shifter(shape):
    cols = shape[1]
    lane = lax.broadcasted_iota(jnp.int32, shape, 1)

    def shifted(x, b):
        if b == 2:
            return x
        out = pltpu.roll(x, (2 - b) % cols, 1)
        valid = lane >= 2 - b if b < 2 else lane < cols + 2 - b
        return jnp.where(valid, out, 0.0)

    return shifted


def closer(shape):
    span = shape[0] // 2
    last = lax.axis_index("tm") == lax.axis_size("tm") - 1
    time = lax.broadcasted_iota(jnp.int32, shape, 0)
    keep = jnp.logical_not(jnp.logical_and(last, time >= span))

    def closed(x):
        return jnp.where(keep, x, 0.0).astype(BF16).astype(F32)

    return closed


def build_slab(slab, x, turn, shifted):
    double = x.shape[0]
    for b in range(5):
        moved = shifted(x, b)
        turn[b] = moved
        for f in range(4):
            piece = moved[: double - 16] if f == 0 else turn[b, SHIFT * f : SHIFT * f + double - 16, :]
            slab[f, b] = piece.astype(BF16)


def inner_kernel(filt_ref, coef_ref, moved_ref, part_ref, white_ref, slab_ref, coefs, turn):
    rows, double, cols = filt_ref.shape
    spots = coef_ref.shape[0] // rows
    shifted = shifter((double, cols))
    closed = closer((double, cols))
    for r in range(rows):
        coefs[r, 0:spots] = coef_ref[pl.ds(r, spots, stride=rows), :]

    def spread(r, _):
        x = filt_ref[r].astype(F32)
        for b in range(5):
            moved_ref[b, r] = shifted(x, b)
        return 0

    lax.fori_loop(0, rows, spread, 0)

    def sums(r):
        total = jnp.zeros((double, cols), F32)
        for a in range(5):
            if 0 <= r + a - 2 < rows:
                for b in range(5):
                    s = 5 * a + b
                    total = total + coefs[r, s : s + 1, :] * moved_ref[b, r + a - 2]
        return total

    for k, r in enumerate((0, 1, rows - 2, rows - 1)):
        part_ref[k] = sums(r)
    for r in range(2, rows - 2):
        white_ref[r - 2] = closed(sums(r))
    build_slab(slab_ref.at[0], white_ref[1], turn, shifted)
    build_slab(slab_ref.at[1], white_ref[3], turn, shifted)
    build_slab(slab_ref.at[2], white_ref[0] - white_ref[1], turn, shifted)
    build_slab(slab_ref.at[3], white_ref[2] - white_ref[3], turn, shifted)
    build_slab(slab_ref.at[4], white_ref[2] - white_ref[1], turn, shifted)


def inner(filt, coef):
    rows, double, cols = filt.shape
    return pl.pallas_call(
        inner_kernel,
        out_shape=(
            jax.ShapeDtypeStruct((5, rows, double, cols), F32),
            jax.ShapeDtypeStruct((4, double, cols), F32),
            jax.ShapeDtypeStruct((rows - 4, double, cols), F32),
            jax.ShapeDtypeStruct((5, 4, 5, double - 16, cols), BF16),
        ),
        in_specs=[vmem()] * 2,
        out_specs=(vmem(),) * 4,
        scratch_shapes=[pltpu.VMEM((rows, 32, cols), F32), pltpu.VMEM((5, double, cols), F32)],
        compiler_params=params(12),
        cost_estimate=pl.CostEstimate(flops=10**9, bytes_accessed=10**7, transcendentals=0),
        name="inner",
    )(filt, coef)


def match_kernel(
    moved_ref,
    part_ref,
    mid_ref,
    mid_slab_ref,
    first_ref,
    second_ref,
    coef_ref,
    sum_ref,
    even_ref,
    odd_ref,
    white_ref,
    best_ref,
    halo,
    coefs,
    edge,
    white,
    turn,
    slabs,
    natural,
    peaks,
):
    rows, double, cols = moved_ref.shape[1:]
    span = double // 2
    half = rows // 2
    spots = coef_ref.shape[0] // rows
    base = half * double
    shifted = shifter((double, cols))
    closed = closer((double, cols))
    upper = lax.rem(lax.axis_index("rows"), 2) == 0

    for side, below in ((first_ref, upper), (second_ref, jnp.logical_not(upper))):
        dest = jnp.where(below, half, 0)

        def spread(k, _, side=side, dest=dest):
            x = side[pl.ds(pl.multiple_of(k * double, double), double), :].astype(F32)
            for b in range(5):
                halo[b, dest + k] = shifted(x, b)
            return 0

        lax.fori_loop(0, half, spread, 0)
        corner = jnp.where(below, 2, 0)
        for k in range(2):
            high = side[base + 64 * k : base + 64 * k + 32, :].astype(F32)
            low = side[base + 64 * k + 32 : base + 64 * k + 64, :].astype(F32)
            edge[corner + k] = high + low
    for k, r in enumerate((0, 1, rows - 2, rows - 1)):
        coefs[k, 0:spots] = coef_ref[pl.ds(r, spots, stride=rows), :]

    def line(b, row):
        if row < half:
            return halo[b, row]
        if row < half + rows:
            return moved_ref[b, row - half]
        return halo[b, row - rows]

    def outside(row):
        return row < half or row >= half + rows

    def sums(w):
        if w < 2 or w >= rows + 2:
            weights, total = edge.at[w if w < 2 else w - rows], jnp.zeros((double, cols), F32)
            offsets = range(5)
        else:
            k = w - 2 if w < 4 else w - rows + 2
            weights, total = coefs.at[k], part_ref[k]
            offsets = [a for a in range(5) if outside(w + a)]
        for a in offsets:
            for b in range(5):
                s = 5 * a + b
                total = total + weights[s : s + 1, :] * line(b, w + a)
        return closed(total)

    for w in (0, 1, 2, 3, rows, rows + 1, rows + 2, rows + 3):
        white[w] = sums(w)
    for w in range(4, rows):
        white[w] = mid_ref[w - 4]
    for r in range(rows):
        natural[pl.ds(r, span, stride=rows), :] = white[r + 2, 0:span]
    white_ref[...] = natural[...].astype(BF16)

    plain, level, step = {}, {}, {}
    plain[2], plain[3], level[2], level[3], step[2] = (mid_slab_ref.at[k] for k in range(5))
    spare = iter(range(12))
    for i in (0, 1, 4, 5):
        plain[i] = slabs.at[next(spare)]
        build_slab(plain[i], white[2 * i + 1], turn, shifted)
        level[i] = slabs.at[next(spare)]
        build_slab(level[i], white[2 * i] - white[2 * i + 1], turn, shifted)
    for i in (0, 1, 3, 4):
        step[i] = slabs.at[next(spare)]
        build_slab(step[i], white[2 * i + 2] - white[2 * i + 1], turn, shifted)

    def score(i, _):
        f = lax.rem(i, 4)
        start = pl.multiple_of(lax.div(i, 4) * 16, 16)

        def product(lhs_ref, source, m, depth):
            blank = [jnp.zeros((64, cols), BF16)] * (depth % 2)
            columns = [
                jnp.concatenate(
                    [source[m + k + j][f, b, pl.ds(start, 64), :] for j in range(depth) for b in range(5)] + blank,
                    axis=0,
                )
                for k in range(2)
            ]
            return jnp.dot(lhs_ref[...], jnp.concatenate(columns, axis=1), preferred_element_type=F32)

        def tiled(found):
            return found.reshape(found.shape[0] // 8, 8, 2 * cols)

        def top(found):
            high = jnp.max(found, axis=0)
            return jnp.maximum(high, pltpu.roll(high, 4, 0))

        for m in range(0, half, 2):
            shared = tiled(product(sum_ref, plain, m, 3))
            upper_row = top(tiled(product(even_ref, level, m, 3)) + shared)
            lower_row = top(tiled(product(odd_ref, step, m, 2)) + shared)
            for k in range(2):
                peaks[i, 2 * (m + k)] = upper_row[:, cols * k : cols * (k + 1)]
                peaks[i, 2 * (m + k) + 1] = lower_row[:, cols * k : cols * (k + 1)]
        return 0

    steps = span // SHIFT
    lax.fori_loop(0, steps, score, 0)
    for i in range(steps):
        for r in range(rows):
            best_ref[pl.ds(SHIFT * rows * i + r, SHIFT, stride=rows), :] = peaks[i, r, 0:SHIFT, :]


def match(inside, first, second, coef, bands):
    moved, part, mid, mid_slabs = inside
    rows, double, cols = moved.shape[1:]
    span = double // 2
    return pl.pallas_call(
        match_kernel,
        out_shape=(
            jax.ShapeDtypeStruct((span * rows, cols), BF16),
            jax.ShapeDtypeStruct((span * rows, cols), F32),
        ),
        in_specs=[vmem()] * 10,
        out_specs=(vmem(), vmem()),
        scratch_shapes=[
            pltpu.VMEM((5, rows, double, cols), F32),
            pltpu.VMEM((4, 32, cols), F32),
            pltpu.VMEM((4, 32, cols), F32),
            pltpu.VMEM((rows + 4, double, cols), F32),
            pltpu.VMEM((5, double, cols), F32),
            pltpu.VMEM((12, 4, 5, double - 16, cols), BF16),
            pltpu.VMEM((span * rows, cols), F32),
            pltpu.VMEM((span // SHIFT, rows, 8, cols), F32),
        ],
        compiler_params=params(24),
        cost_estimate=pl.CostEstimate(flops=11 * 10**9, bytes_accessed=10**7, transcendentals=0),
        name="match",
    )(moved, part, mid, mid_slabs, first, second, coef, *bands)


def shards(raw_signal, fir_taps, white_coef, templates):
    span, rows, cols = raw_signal.shape
    raw = raw_signal.reshape(span * rows, cols)
    coef = white_coef.reshape(-1, cols)
    far, raw = opening(raw, rows, fir_taps.shape[0])
    far = swap_pairs(far, "tm", 1)
    near = swap_pairs(raw, "tm", 0)
    band, *bands, coef = prep(fir_taps, templates, coef, span)
    filt, first, second = fir(band, raw, near, far, coef, rows)
    first = swap_pairs(first, "rows", 0)
    second = swap_pairs(second, "rows", 1)
    inside = inner(filt, coef)
    whitened, best = match(inside, first, second, coef, bands)
    return whitened.reshape(span, rows, cols), best.reshape(span, rows, cols)


def solution(mesh):
    return jax.shard_map(
        shards,
        mesh=mesh,
        in_specs=(P("tm", "rows", None), P(), P(None, "rows", None), P()),
        out_specs=(P("tm", "rows", None), P("tm", "rows", None)),
        check_vma=False,
    )
```

```python
import jax
import jax.numpy as jnp
from jax import lax
from jax.experimental import pallas as pl
from jax.experimental.pallas import tpu as pltpu
from jax.sharding import PartitionSpec as P


F32 = jnp.float32
BF16 = jnp.bfloat16
SHIFT = 4


def vmem():
    return pl.BlockSpec(memory_space=pltpu.VMEM)


def params(mib):
    return pltpu.CompilerParams(vmem_limit_bytes=mib * 1024 * 1024)


def swap_pairs(array, axis, first):
    size = lax.axis_size(axis)
    pairs = []
    for low in range(first, size - 1, 2):
        pairs += [(low, low + 1), (low + 1, low)]
    return lax.ppermute(array, axis, pairs)


def open_kernel(raw_ref, far_ref, keep_ref):
    skip = raw_ref.shape[0] - far_ref.shape[0]
    even = lax.rem(lax.axis_index("tm"), 2) == 0
    start = pl.multiple_of(jnp.where(even, 0, skip), 16)
    far_ref[...] = raw_ref[pl.ds(start, far_ref.shape[0]), :].astype(BF16)
    keep_ref[...] = raw_ref[...]


def opening(raw, rows, taps):
    return pl.pallas_call(
        open_kernel,
        out_shape=(
            jax.ShapeDtypeStruct(((taps - 1) * rows, raw.shape[1]), BF16),
            jax.ShapeDtypeStruct(raw.shape, F32),
        ),
        in_specs=[vmem()],
        out_specs=(vmem(), vmem()),
        compiler_params=params(4),
        cost_estimate=pl.CostEstimate(flops=10**5, bytes_accessed=10**6, transcendentals=0),
        name="opening",
    )(raw)


def prep_kernel(
    line_ref, tmpl_ref, coef_in_ref, band_ref, sum_ref, even_ref, odd_ref, coef_ref, wide, mixed
):
    coef_ref[...] = coef_in_ref[...]
    spots, count, length = tmpl_ref.shape
    rows = band_ref.shape[0]
    line = jnp.broadcast_to(line_ref[...], (rows, 256))
    band = pltpu.roll(line, 0, 1, stride=1, stride_axis=0)
    high = band.astype(BF16)
    low = (band - high.astype(F32)).astype(BF16)
    band_ref[:, 0:256] = high
    band_ref[:, 256:512] = low
    band_ref[:, 512:768] = high

    wide[...] = jnp.zeros_like(wide)
    for s in range(spots):
        wide[s, :, 0:length] = tmpl_ref[s].astype(F32)

    def even_spot(k):
        return wide[10 * (k // 5) + k % 5]

    def odd_spot(k):
        return wide[10 * (k // 5) + 5 + k % 5]

    def both_spots(k):
        return even_spot(k) + odd_spot(k) if k < 10 else even_spot(k)

    slot = 0
    for out_ref, piece, size in ((sum_ref, both_spots, 15), (even_ref, even_spot, 15), (odd_ref, odd_spot, 10)):
        for p in range(0, size, 2):
            pair = piece(p)
            if p + 1 < size:
                pair = pair + pltpu.roll(piece(p + 1), 64, 1)
            for b in range(SHIFT):
                moved = pltpu.roll(pair, b, 1) if b else pair
                mixed[slot, pl.ds(b, count, stride=SHIFT), :] = moved
            out_ref[:, 64 * p : 64 * p + 128] = mixed[slot].astype(BF16)
            slot += 1


def prep(fir_taps, templates, coef, span):
    count, _, spots = templates.shape
    taps = fir_taps.shape[0]
    line = jnp.pad(fir_taps[::-1], (span - taps + 1, 255 - span))[None]
    by_spot = jnp.transpose(templates, (2, 0, 1))
    return pl.pallas_call(
        prep_kernel,
        out_shape=(
            jax.ShapeDtypeStruct((2 * span, 768), BF16),
            jax.ShapeDtypeStruct((count * SHIFT, 16 * 64), BF16),
            jax.ShapeDtypeStruct((count * SHIFT, 16 * 64), BF16),
            jax.ShapeDtypeStruct((count * SHIFT, 10 * 64), BF16),
            jax.ShapeDtypeStruct(coef.shape, F32),
        ),
        in_specs=[vmem()] * 3,
        out_specs=(vmem(),) * 5,
        scratch_shapes=[
            pltpu.VMEM((spots, count, 128), F32),
            pltpu.VMEM((21, count * SHIFT, 128), F32),
        ],
        compiler_params=params(8),
        cost_estimate=pl.CostEstimate(flops=10**7, bytes_accessed=2 * 10**6, transcendentals=0),
        name="prep",
    )(line, by_spot, coef)


def fir_kernel(band_ref, raw_ref, near_ref, far_ref, coef_ref, filt_ref, first_ref, second_ref, widened):
    rows, double, cols = filt_ref.shape
    span = double // 2
    half = rows // 2
    even = lax.rem(lax.axis_index("tm"), 2) == 0
    short = far_ref.shape[0]
    skip = widened.shape[0] - short
    widened[0:skip, :] = jnp.zeros((skip, cols), F32)
    widened[short:, :] = jnp.zeros((skip, cols), F32)
    widened[pl.ds(pl.multiple_of(jnp.where(even, skip, 0), 16), short), :] = far_ref[...].astype(F32)
    columns = []
    for r in range(rows):
        near = near_ref[pl.ds(r, span, stride=rows), :]
        far = widened[pl.ds(r, span, stride=rows), :]
        own = raw_ref[pl.ds(r, span, stride=rows), :]
        before = jnp.where(even, far, near)
        after = jnp.where(even, near, far)
        line = jnp.concatenate([before, own, after, jnp.zeros_like(own)], axis=0)
        high = line.astype(BF16)
        low = (line - high.astype(F32)).astype(BF16)
        columns.append(jnp.concatenate([high, high, low], axis=0))
    for r in range(0, rows, 2):
        pair = jnp.concatenate(columns[r : r + 2], axis=1)
        out = jnp.dot(band_ref[...], pair, preferred_element_type=F32).astype(BF16)
        filt_ref[r] = out[:, :cols]
        filt_ref[r + 1] = out[:, cols:]
    spots = coef_ref.shape[0] // rows
    base = half * double
    upper = lax.rem(lax.axis_index("rows"), 2) == 0
    for side, at_end in ((first_ref, upper), (second_ref, jnp.logical_not(upper))):
        start = jnp.where(at_end, half, 0)
        for k in range(half):
            side[double * k : double * (k + 1), :] = filt_ref[start + k]
        side[base : base + 128, :] = jnp.zeros((128, cols), BF16)
        edge = jnp.where(at_end, rows - 2, 0)
        for k in range(2):
            coef = coef_ref[pl.ds(edge + k, spots, stride=rows), :]
            high = coef.astype(BF16)
            low = (coef - high.astype(F32)).astype(BF16)
            side[base + 64 * k : base + 64 * k + spots, :] = high
            side[base + 64 * k + 32 : base + 64 * k + 32 + spots, :] = low


def fir(band, raw, near, far, coef, rows):
    span = raw.shape[0] // rows
    cols = raw.shape[1]
    message = jax.ShapeDtypeStruct((rows // 2 * 2 * span + 128, cols), BF16)
    return pl.pallas_call(
        fir_kernel,
        out_shape=(jax.ShapeDtypeStruct((rows, 2 * span, cols), BF16), message, message),
        in_specs=[vmem()] * 5,
        out_specs=(vmem(),) * 3,
        scratch_shapes=[pltpu.VMEM(raw.shape, F32)],
        compiler_params=params(8),
        cost_estimate=pl.CostEstimate(flops=2 * 10**8, bytes_accessed=2 * 10**6, transcendentals=0),
        name="fir",
    )(band, raw, near, far, coef)


def shifter(shape):
    cols = shape[1]
    lane = lax.broadcasted_iota(jnp.int32, shape, 1)

    def shifted(x, b):
        if b == 2:
            return x
        out = pltpu.roll(x, (2 - b) % cols, 1)
        valid = lane >= 2 - b if b < 2 else lane < cols + 2 - b
        return jnp.where(valid, out, 0.0)

    return shifted


def closer(shape):
    span = shape[0] // 2
    last = lax.axis_index("tm") == lax.axis_size("tm") - 1
    time = lax.broadcasted_iota(jnp.int32, shape, 0)
    keep = jnp.logical_not(jnp.logical_and(last, time >= span))

    def closed(x):
        return jnp.where(keep, x, 0.0).astype(BF16).astype(F32)

    return closed


def build_slab(slab, x, turn, shifted):
    double = x.shape[0]
    for b in range(5):
        moved = shifted(x, b)
        turn[b] = moved
        for f in range(4):
            piece = moved[: double - 16] if f == 0 else turn[b, SHIFT * f : SHIFT * f + double - 16, :]
            slab[f, b] = piece.astype(BF16)


def inner_kernel(filt_ref, coef_ref, moved_ref, part_ref, white_ref, slab_ref, coefs, turn):
    rows, double, cols = filt_ref.shape
    spots = coef_ref.shape[0] // rows
    shifted = shifter((double, cols))
    closed = closer((double, cols))
    for r in range(rows):
        coefs[r, 0:spots] = coef_ref[pl.ds(r, spots, stride=rows), :]

    def spread(r, _):
        x = filt_ref[r].astype(F32)
        for b in range(5):
            moved_ref[b, r] = shifted(x, b)
        return 0

    lax.fori_loop(0, rows, spread, 0)

    def sums(r):
        total = jnp.zeros((double, cols), F32)
        for a in range(5):
            if 0 <= r + a - 2 < rows:
                for b in range(5):
                    s = 5 * a + b
                    total = total + coefs[r, s : s + 1, :] * moved_ref[b, r + a - 2]
        return total

    for k, r in enumerate((0, 1, rows - 2, rows - 1)):
        part_ref[k] = sums(r)
    for r in range(2, rows - 2):
        white_ref[r - 2] = closed(sums(r))
    build_slab(slab_ref.at[0], white_ref[1], turn, shifted)
    build_slab(slab_ref.at[1], white_ref[3], turn, shifted)
    build_slab(slab_ref.at[2], white_ref[0] - white_ref[1], turn, shifted)
    build_slab(slab_ref.at[3], white_ref[2] - white_ref[3], turn, shifted)
    build_slab(slab_ref.at[4], white_ref[2] - white_ref[1], turn, shifted)


def inner(filt, coef):
    rows, double, cols = filt.shape
    return pl.pallas_call(
        inner_kernel,
        out_shape=(
            jax.ShapeDtypeStruct((5, rows, double, cols), F32),
            jax.ShapeDtypeStruct((4, double, cols), F32),
            jax.ShapeDtypeStruct((rows - 4, double, cols), F32),
            jax.ShapeDtypeStruct((5, 4, 5, double - 16, cols), BF16),
        ),
        in_specs=[vmem()] * 2,
        out_specs=(vmem(),) * 4,
        scratch_shapes=[pltpu.VMEM((rows, 32, cols), F32), pltpu.VMEM((5, double, cols), F32)],
        compiler_params=params(12),
        cost_estimate=pl.CostEstimate(flops=10**9, bytes_accessed=10**7, transcendentals=0),
        name="inner",
    )(filt, coef)


def match_kernel(
    moved_ref,
    part_ref,
    mid_ref,
    mid_slab_ref,
    first_ref,
    second_ref,
    coef_ref,
    sum_ref,
    even_ref,
    odd_ref,
    white_hbm,
    best_hbm,
    halo,
    coefs,
    edge,
    white,
    turn,
    slabs,
    natural,
    rounded,
    best,
    sems,
):
    rows, double, cols = moved_ref.shape[1:]
    span = double // 2
    half = rows // 2
    spots = coef_ref.shape[0] // rows
    base = half * double
    shifted = shifter((double, cols))
    closed = closer((double, cols))
    upper = lax.rem(lax.axis_index("rows"), 2) == 0

    for side, below in ((first_ref, upper), (second_ref, jnp.logical_not(upper))):
        dest = jnp.where(below, half, 0)

        def spread(k, _, side=side, dest=dest):
            x = side[pl.ds(pl.multiple_of(k * double, double), double), :].astype(F32)
            for b in range(5):
                halo[b, dest + k] = shifted(x, b)
            return 0

        lax.fori_loop(0, half, spread, 0)
        corner = jnp.where(below, 2, 0)
        for k in range(2):
            high = side[base + 64 * k : base + 64 * k + 32, :].astype(F32)
            low = side[base + 64 * k + 32 : base + 64 * k + 64, :].astype(F32)
            edge[corner + k] = high + low
    for k, r in enumerate((0, 1, rows - 2, rows - 1)):
        coefs[k, 0:spots] = coef_ref[pl.ds(r, spots, stride=rows), :]

    def line(b, row):
        if row < half:
            return halo[b, row]
        if row < half + rows:
            return moved_ref[b, row - half]
        return halo[b, row - rows]

    def outside(row):
        return row < half or row >= half + rows

    def sums(w):
        if w < 2 or w >= rows + 2:
            weights, total = edge.at[w if w < 2 else w - rows], jnp.zeros((double, cols), F32)
            offsets = range(5)
        else:
            k = w - 2 if w < 4 else w - rows + 2
            weights, total = coefs.at[k], part_ref[k]
            offsets = [a for a in range(5) if outside(w + a)]
        for a in offsets:
            for b in range(5):
                s = 5 * a + b
                total = total + weights[s : s + 1, :] * line(b, w + a)
        return closed(total)

    for w in (0, 1, 2, 3, rows, rows + 1, rows + 2, rows + 3):
        white[w] = sums(w)
    for w in range(4, rows):
        white[w] = mid_ref[w - 4]
    for r in range(rows):
        natural[pl.ds(r, span, stride=rows), :] = white[r + 2, 0:span]
    rounded[...] = natural[...].astype(BF16)
    white_copy = pltpu.make_async_copy(rounded, white_hbm, sems.at[span // (4 * SHIFT)])
    white_copy.start()

    plain, level, step = {}, {}, {}
    plain[2], plain[3], level[2], level[3], step[2] = (mid_slab_ref.at[k] for k in range(5))
    spare = iter(range(12))
    for i in (0, 1, 4, 5):
        plain[i] = slabs.at[next(spare)]
        build_slab(plain[i], white[2 * i + 1], turn, shifted)
        level[i] = slabs.at[next(spare)]
        build_slab(level[i], white[2 * i] - white[2 * i + 1], turn, shifted)
    for i in (0, 1, 3, 4):
        step[i] = slabs.at[next(spare)]
        build_slab(step[i], white[2 * i + 2] - white[2 * i + 1], turn, shifted)

    def product(lhs_ref, source, f, start, depth):
        blank = [jnp.zeros((64, cols), BF16)] * (depth % 2)
        columns = [
            jnp.concatenate(
                [source[m + j][f, b, pl.ds(start, 64), :] for j in range(depth) for b in range(5)] + blank, axis=0
            )
            for m in range(half)
        ]
        found = jnp.dot(lhs_ref[...], jnp.concatenate(columns, axis=1), preferred_element_type=F32)
        return found.reshape(found.shape[0] // 8, 8, half * cols)

    def top(found):
        high = jnp.max(found, axis=0)
        return jnp.maximum(high, pltpu.roll(high, 4, 0))

    chunk = 4 * SHIFT * rows

    def sent(q):
        part = pl.ds(pl.multiple_of(q * chunk, chunk), chunk)
        return pltpu.make_async_copy(best.at[part, :], best_hbm.at[part, :], sems.at[q])

    def score(q, _):
        start = pl.multiple_of(q * 16, 16)
        for f in range(4):
            shared = product(sum_ref, plain, f, start, 3)
            found = (
                top(product(even_ref, level, f, start, 3) + shared),
                top(product(odd_ref, step, f, start, 2) + shared),
            )
            for r in range(rows):
                first_row = q * chunk + SHIFT * rows * f + r
                m = r // 2
                best[pl.ds(first_row, SHIFT, stride=rows), :] = found[r % 2][0:SHIFT, cols * m : cols * (m + 1)]
        sent(q).start()
        return 0

    parts = span // (4 * SHIFT)
    lax.fori_loop(0, parts, score, 0)
    for q in range(parts):
        sent(q).wait()
    white_copy.wait()


def match(inside, first, second, coef, bands):
    moved, part, mid, mid_slabs = inside
    rows, double, cols = moved.shape[1:]
    span = double // 2
    return pl.pallas_call(
        match_kernel,
        out_shape=(
            jax.ShapeDtypeStruct((span * rows, cols), BF16),
            jax.ShapeDtypeStruct((span * rows, cols), F32),
        ),
        in_specs=[vmem()] * 10,
        out_specs=(pl.BlockSpec(memory_space=pltpu.HBM),) * 2,
        scratch_shapes=[
            pltpu.VMEM((5, rows, double, cols), F32),
            pltpu.VMEM((4, 32, cols), F32),
            pltpu.VMEM((4, 32, cols), F32),
            pltpu.VMEM((rows + 4, double, cols), F32),
            pltpu.VMEM((5, double, cols), F32),
            pltpu.VMEM((12, 4, 5, double - 16, cols), BF16),
            pltpu.VMEM((span * rows, cols), F32),
            pltpu.VMEM((span * rows, cols), BF16),
            pltpu.VMEM((span * rows, cols), F32),
            pltpu.SemaphoreType.DMA((span // (4 * SHIFT) + 1,)),
        ],
        compiler_params=params(24),
        cost_estimate=pl.CostEstimate(flops=11 * 10**9, bytes_accessed=10**7, transcendentals=0),
        name="match",
    )(moved, part, mid, mid_slabs, first, second, coef, *bands)


def shards(raw_signal, fir_taps, white_coef, templates):
    span, rows, cols = raw_signal.shape
    raw = raw_signal.reshape(span * rows, cols)
    coef = white_coef.reshape(-1, cols)
    far, raw = opening(raw, rows, fir_taps.shape[0])
    far = swap_pairs(far, "tm", 1)
    near = swap_pairs(raw, "tm", 0)
    band, *bands, coef = prep(fir_taps, templates, coef, span)
    filt, first, second = fir(band, raw, near, far, coef, rows)
    first = swap_pairs(first, "rows", 0)
    second = swap_pairs(second, "rows", 1)
    inside = inner(filt, coef)
    whitened, best = match(inside, first, second, coef, bands)
    return whitened.reshape(span, rows, cols), best.reshape(span, rows, cols)


def solution(mesh):
    return jax.shard_map(
        shards,
        mesh=mesh,
        in_specs=(P("tm", "rows", None), P(), P(None, "rows", None), P()),
        out_specs=(P("tm", "rows", None), P("tm", "rows", None)),
        check_vma=False,
    )
```

```python
import jax
import jax.numpy as jnp
from jax import lax
from jax.experimental import pallas as pl
from jax.experimental.pallas import tpu as pltpu
from jax.sharding import PartitionSpec as P


F32 = jnp.float32
BF16 = jnp.bfloat16
SHIFT = 4


def vmem():
    return pl.BlockSpec(memory_space=pltpu.VMEM)


def params(mib):
    return pltpu.CompilerParams(vmem_limit_bytes=mib * 1024 * 1024)


def swap_pairs(array, axis, first):
    size = lax.axis_size(axis)
    pairs = []
    for low in range(first, size - 1, 2):
        pairs += [(low, low + 1), (low + 1, low)]
    return lax.ppermute(array, axis, pairs)


def is_upper():
    return lax.rem(lax.axis_index("rows"), 2) == 0


def open_kernel(raw_ref, far_ref, keep_ref):
    skip = raw_ref.shape[0] - far_ref.shape[0]
    even = lax.rem(lax.axis_index("tm"), 2) == 0
    start = pl.multiple_of(jnp.where(even, 0, skip), 16)
    far_ref[...] = raw_ref[pl.ds(start, far_ref.shape[0]), :].astype(BF16)
    keep_ref[...] = raw_ref[...]


def opening(raw, rows, taps):
    return pl.pallas_call(
        open_kernel,
        out_shape=(
            jax.ShapeDtypeStruct(((taps - 1) * rows, raw.shape[1]), BF16),
            jax.ShapeDtypeStruct(raw.shape, F32),
        ),
        in_specs=[vmem()],
        out_specs=(vmem(), vmem()),
        compiler_params=params(4),
        cost_estimate=pl.CostEstimate(flops=10**5, bytes_accessed=10**6, transcendentals=0),
        name="opening",
    )(raw)


def prep_kernel(
    line_ref, tmpl_ref, coef_in_ref, band_ref, sum_ref, even_ref, odd_ref, coef_ref, wide, mixed
):
    _, count, length = tmpl_ref.shape
    own_rows = coef_ref.shape[0]
    upper = is_upper()
    for a in range(5):
        source = jnp.where(upper, a, 4 - a) * (5 * own_rows)
        for r in range(own_rows):
            line = pl.ds(source + jnp.where(upper, r, own_rows - 1 - r), 5, stride=own_rows)
            coef_ref[r, 5 * a : 5 * a + 5, :] = coef_in_ref[line, :]
    rows = band_ref.shape[0]
    line = jnp.broadcast_to(line_ref[...], (rows, 256))
    band = pltpu.roll(line, 0, 1, stride=1, stride_axis=0)
    high = band.astype(BF16)
    low = (band - high.astype(F32)).astype(BF16)
    band_ref[:, 0:256] = high
    band_ref[:, 256:512] = low
    band_ref[:, 512:768] = high

    wide[...] = jnp.zeros_like(wide)
    for a in range(5):
        source = jnp.where(upper, a, 4 - a) * 5
        for b in range(5):
            wide[5 * a + b, :, 0:length] = tmpl_ref[source + b].astype(F32)

    def even_spot(k):
        return wide[10 * (k // 5) + k % 5]

    def odd_spot(k):
        return wide[10 * (k // 5) + 5 + k % 5]

    def both_spots(k):
        return even_spot(k) + odd_spot(k) if k < 10 else even_spot(k)

    slot = 0
    for out_ref, piece, size in ((sum_ref, both_spots, 15), (even_ref, even_spot, 15), (odd_ref, odd_spot, 10)):
        for p in range(0, size, 2):
            pair = piece(p)
            if p + 1 < size:
                pair = pair + pltpu.roll(piece(p + 1), 64, 1)
            for b in range(SHIFT):
                moved = pltpu.roll(pair, b, 1) if b else pair
                mixed[slot, pl.ds(b, count, stride=SHIFT), :] = moved
            out_ref[:, 64 * p : 64 * p + 128] = mixed[slot].astype(BF16)
            slot += 1


def prep(fir_taps, templates, coef, span, rows):
    count, _, spots = templates.shape
    taps = fir_taps.shape[0]
    line = jnp.pad(fir_taps[::-1], (span - taps + 1, 255 - span))[None]
    by_spot = jnp.transpose(templates, (2, 0, 1))
    return pl.pallas_call(
        prep_kernel,
        out_shape=(
            jax.ShapeDtypeStruct((2 * span, 768), BF16),
            jax.ShapeDtypeStruct((count * SHIFT, 16 * 64), BF16),
            jax.ShapeDtypeStruct((count * SHIFT, 16 * 64), BF16),
            jax.ShapeDtypeStruct((count * SHIFT, 10 * 64), BF16),
            jax.ShapeDtypeStruct((rows, 32, coef.shape[1]), F32),
        ),
        in_specs=[vmem()] * 3,
        out_specs=(vmem(),) * 5,
        scratch_shapes=[
            pltpu.VMEM((spots, count, 128), F32),
            pltpu.VMEM((21, count * SHIFT, 128), F32),
        ],
        compiler_params=params(8),
        cost_estimate=pl.CostEstimate(flops=10**7, bytes_accessed=2 * 10**6, transcendentals=0),
        name="prep",
    )(line, by_spot, coef)


def fir_kernel(band_ref, raw_ref, near_ref, far_ref, coef_ref, filt_ref, first_ref, second_ref, widened, block):
    rows, double, cols = filt_ref.shape
    span = double // 2
    half = rows // 2
    even = lax.rem(lax.axis_index("tm"), 2) == 0
    short = far_ref.shape[0]
    skip = widened.shape[0] - short
    widened[0:skip, :] = jnp.zeros((skip, cols), F32)
    widened[short:, :] = jnp.zeros((skip, cols), F32)
    widened[pl.ds(pl.multiple_of(jnp.where(even, skip, 0), 16), short), :] = far_ref[...].astype(F32)
    columns = []
    upper = is_upper()
    for r in range(rows):
        line = pl.ds(jnp.where(upper, r, rows - 1 - r), span, stride=rows)
        near = near_ref[line, :]
        far = widened[line, :]
        own = raw_ref[line, :]
        before = jnp.where(even, far, near)
        after = jnp.where(even, near, far)
        line = jnp.concatenate([before, own, after, jnp.zeros_like(own)], axis=0)
        high = line.astype(BF16)
        low = (line - high.astype(F32)).astype(BF16)
        columns.append(jnp.concatenate([high, high, low], axis=0))
    for r in range(0, rows, 2):
        pair = jnp.concatenate(columns[r : r + 2], axis=1)
        out = jnp.dot(band_ref[...], pair, preferred_element_type=F32).astype(BF16)
        filt_ref[r] = out[:, :cols]
        filt_ref[r + 1] = out[:, cols:]
    base = half * double
    for side, order, edge in (
        (first_ref, range(rows - 1, rows - half - 1, -1), (rows - 1, rows - 2)),
        (second_ref, range(half - 1, -1, -1), (1, 0)),
    ):
        for k, r in enumerate(order):
            side[double * k : double * (k + 1), :] = filt_ref[r]
        for k, r in enumerate(edge):
            block[...] = jnp.zeros_like(block)
            for a in range(5):
                block[5 * a : 5 * a + 5, :] = coef_ref[r, 20 - 5 * a : 25 - 5 * a, :]
            high = block[...].astype(BF16)
            side[base + 64 * k : base + 64 * k + 32, :] = high
            side[base + 64 * k + 32 : base + 64 * k + 64, :] = (block[...] - high.astype(F32)).astype(BF16)


def fir(band, raw, near, far, coef, rows):
    span = raw.shape[0] // rows
    cols = raw.shape[1]
    message = jax.ShapeDtypeStruct((rows // 2 * 2 * span + 128, cols), BF16)
    return pl.pallas_call(
        fir_kernel,
        out_shape=(jax.ShapeDtypeStruct((rows, 2 * span, cols), BF16), message, message),
        in_specs=[vmem()] * 5,
        out_specs=(vmem(),) * 3,
        scratch_shapes=[pltpu.VMEM(raw.shape, F32), pltpu.VMEM(coef.shape[1:], F32)],
        compiler_params=params(8),
        cost_estimate=pl.CostEstimate(flops=2 * 10**8, bytes_accessed=2 * 10**6, transcendentals=0),
        name="fir",
    )(band, raw, near, far, coef)


def shifter(shape):
    cols = shape[1]
    lane = lax.broadcasted_iota(jnp.int32, shape, 1)

    def shifted(x, b):
        if b == 2:
            return x
        out = pltpu.roll(x, (2 - b) % cols, 1)
        valid = lane >= 2 - b if b < 2 else lane < cols + 2 - b
        return jnp.where(valid, out, 0.0)

    return shifted


def closer(shape):
    span = shape[0] // 2
    last = lax.axis_index("tm") == lax.axis_size("tm") - 1
    time = lax.broadcasted_iota(jnp.int32, shape, 0)
    keep = jnp.logical_not(jnp.logical_and(last, time >= span))

    def closed(x):
        return jnp.where(keep, x, 0.0).astype(BF16).astype(F32)

    return closed


def build_slab(slab, x, shifted):
    double = x.shape[0]
    for b in range(5):
        moved = shifted(x, b)
        later = pltpu.roll(moved, double - SHIFT, 0)
        for f in range(4):
            piece = (later if f % 2 else moved)[8 * (f // 2) : 8 * (f // 2) + double - 16]
            slab[f, b] = piece.astype(BF16)


def inner_kernel(filt_ref, coef_ref, moved_ref, part_ref, white_ref, slab_ref):
    rows, double, cols = filt_ref.shape
    shifted = shifter((double, cols))
    closed = closer((double, cols))

    def spread(r, _):
        x = filt_ref[r].astype(F32)
        for b in range(5):
            moved_ref[b, r] = shifted(x, b)
        return 0

    lax.fori_loop(0, rows, spread, 0)

    def sums(r):
        total = jnp.zeros((double, cols), F32)
        for a in range(5):
            if 0 <= r + a - 2 < rows:
                for b in range(5):
                    s = 5 * a + b
                    total = total + coef_ref[r, s : s + 1, :] * moved_ref[b, r + a - 2]
        return total

    for k, r in enumerate((0, 1, rows - 2, rows - 1)):
        part_ref[k] = sums(r)
    for r in range(2, rows - 2):
        white_ref[r - 2] = closed(sums(r))
    build_slab(slab_ref.at[0], white_ref[1], shifted)
    build_slab(slab_ref.at[1], white_ref[3], shifted)
    build_slab(slab_ref.at[2], white_ref[0] - white_ref[1], shifted)
    build_slab(slab_ref.at[3], white_ref[2] - white_ref[3], shifted)
    build_slab(slab_ref.at[4], white_ref[2] - white_ref[1], shifted)


def inner(filt, coef):
    rows, double, cols = filt.shape
    return pl.pallas_call(
        inner_kernel,
        out_shape=(
            jax.ShapeDtypeStruct((5, rows, double, cols), F32),
            jax.ShapeDtypeStruct((4, double, cols), F32),
            jax.ShapeDtypeStruct((rows - 4, double, cols), F32),
            jax.ShapeDtypeStruct((5, 4, 5, double - 16, cols), BF16),
        ),
        in_specs=[vmem()] * 2,
        out_specs=(vmem(),) * 4,
        compiler_params=params(12),
        cost_estimate=pl.CostEstimate(flops=10**9, bytes_accessed=10**7, transcendentals=0),
        name="inner",
    )(filt, coef)


def spread_halo(side, halo, edge, shifted):
    half, double = halo.shape[1:3]

    def spread(k, _):
        x = side[pl.ds(pl.multiple_of(k * double, double), double), :].astype(F32)
        for b in range(5):
            halo[b, k] = shifted(x, b)
        return 0

    lax.fori_loop(0, half, spread, 0)
    base = half * double
    for k in range(2):
        high = side[base + 64 * k : base + 64 * k + 32, :].astype(F32)
        low = side[base + 64 * k + 32 : base + 64 * k + 64, :].astype(F32)
        edge[k] = high + low


def gather(total, weights, lines):
    for s, piece in lines:
        total = total + weights[s : s + 1, :] * piece
    return total


def after_kernel(side_ref, moved_ref, part_ref, mid_ref, coef_ref, white_ref, slab_ref, halo, edge, white):
    rows, double, cols = moved_ref.shape[1:]
    half = rows // 2
    shifted = shifter((double, cols))
    closed = closer((double, cols))
    spread_halo(side_ref, halo, edge, shifted)

    def lines(w, offsets):
        for a in offsets:
            row = w + a - half
            for b in range(5):
                yield 5 * a + b, moved_ref[b, row] if row < rows else halo[b, row - rows]

    zero = jnp.zeros((double, cols), F32)
    white[0] = closed(gather(part_ref[2], coef_ref.at[rows - 2], lines(rows, (4,))))
    white[1] = closed(gather(part_ref[3], coef_ref.at[rows - 1], lines(rows + 1, (3, 4))))
    white[2] = closed(gather(zero, edge.at[0], lines(rows + 2, range(5))))
    white[3] = closed(gather(zero, edge.at[1], lines(rows + 3, range(5))))
    white_ref[0] = white[0]
    white_ref[1] = white[1]
    build_slab(slab_ref.at[0], white[1], shifted)
    build_slab(slab_ref.at[1], white[3], shifted)
    build_slab(slab_ref.at[2], white[0] - white[1], shifted)
    build_slab(slab_ref.at[3], white[2] - white[3], shifted)
    build_slab(slab_ref.at[4], white[0] - mid_ref[rows - 5], shifted)
    build_slab(slab_ref.at[5], white[2] - white[1], shifted)


def after(side, inside, coef):
    moved, part, mid, _ = inside
    rows, double, cols = moved.shape[1:]
    return pl.pallas_call(
        after_kernel,
        out_shape=(
            jax.ShapeDtypeStruct((2, double, cols), F32),
            jax.ShapeDtypeStruct((6, 4, 5, double - 16, cols), BF16),
        ),
        in_specs=[vmem()] * 5,
        out_specs=(vmem(),) * 2,
        scratch_shapes=[
            pltpu.VMEM((5, rows // 2, double, cols), F32),
            pltpu.VMEM((2, 32, cols), F32),
            pltpu.VMEM((4, double, cols), F32),
        ],
        compiler_params=params(12),
        cost_estimate=pl.CostEstimate(flops=10**9, bytes_accessed=10**7, transcendentals=0),
        name="after",
    )(side, moved, part, mid, coef)


def match_kernel(
    side_ref,
    moved_ref,
    part_ref,
    mid_ref,
    mid_slab_ref,
    low_ref,
    low_slab_ref,
    coef_ref,
    sum_ref,
    even_ref,
    odd_ref,
    white_hbm,
    best_hbm,
    halo,
    edge,
    white,
    slabs,
    natural,
    rounded,
    best,
    sems,
):
    rows, double, cols = moved_ref.shape[1:]
    span = double // 2
    half = rows // 2
    shifted = shifter((double, cols))
    closed = closer((double, cols))
    upper = is_upper()

    def actual(r):
        return jnp.where(upper, r, rows - 1 - r)

    spread_halo(side_ref, halo, edge, shifted)

    def lines(w, offsets):
        for a in offsets:
            row = w + a
            for b in range(5):
                yield 5 * a + b, halo[b, row] if row < half else moved_ref[b, row - half]

    zero = jnp.zeros((double, cols), F32)
    white[0] = closed(gather(zero, edge.at[0], lines(0, range(5))))
    white[1] = closed(gather(zero, edge.at[1], lines(1, range(5))))
    white[2] = closed(gather(part_ref[0], coef_ref.at[0], lines(2, (0, 1))))
    white[3] = closed(gather(part_ref[1], coef_ref.at[1], lines(3, (0,))))
    for r in range(rows):
        if r < 2:
            line = white[r + 2, 0:span]
        elif r < rows - 2:
            line = mid_ref[r - 2, 0:span]
        else:
            line = low_ref[r - rows + 2, 0:span]
        natural[pl.ds(actual(r), span, stride=rows), :] = line
    rounded[...] = natural[...].astype(BF16)
    white_copy = pltpu.make_async_copy(rounded, white_hbm, sems.at[span // (4 * SHIFT)])
    white_copy.start()

    build_slab(slabs.at[0], white[1], shifted)
    build_slab(slabs.at[1], white[3], shifted)
    build_slab(slabs.at[2], white[0] - white[1], shifted)
    build_slab(slabs.at[3], white[2] - white[3], shifted)
    build_slab(slabs.at[4], white[2] - white[1], shifted)
    build_slab(slabs.at[5], mid_ref[0] - white[3], shifted)
    high = [slabs.at[k] for k in range(6)]
    mid = [mid_slab_ref.at[k] for k in range(5)]
    low = [low_slab_ref.at[k] for k in range(6)]
    plain = high[0:2] + mid[0:2] + low[0:2]
    level = high[2:4] + mid[2:4] + low[2:4]
    step = high[4:6] + mid[4:5] + low[4:6]

    def product(lhs_ref, source, f, start, depth):
        blank = [jnp.zeros((64, cols), BF16)] * (depth % 2)
        columns = [
            jnp.concatenate(
                [source[m + j][f, b, pl.ds(start, 64), :] for j in range(depth) for b in range(5)] + blank, axis=0
            )
            for m in range(half)
        ]
        found = jnp.dot(lhs_ref[...], jnp.concatenate(columns, axis=1), preferred_element_type=F32)
        return found.reshape(found.shape[0] // 8, 8, half * cols)

    def top(found):
        high = jnp.max(found, axis=0)
        return jnp.maximum(high, pltpu.roll(high, 4, 0))

    chunk = 4 * SHIFT * rows

    def sent(q):
        part = pl.ds(pl.multiple_of(q * chunk, chunk), chunk)
        return pltpu.make_async_copy(best.at[part, :], best_hbm.at[part, :], sems.at[q])

    def score(q, _):
        start = pl.multiple_of(q * 16, 16)
        for f in range(4):
            shared = product(sum_ref, plain, f, start, 3)
            found = (
                top(product(even_ref, level, f, start, 3) + shared),
                top(product(odd_ref, step, f, start, 2) + shared),
            )
            for r in range(rows):
                first_row = q * chunk + SHIFT * rows * f + actual(r)
                m = r // 2
                best[pl.ds(first_row, SHIFT, stride=rows), :] = found[r % 2][0:SHIFT, cols * m : cols * (m + 1)]
        sent(q).start()
        return 0

    parts = span // (4 * SHIFT)
    lax.fori_loop(0, parts, score, 0)
    for q in range(parts):
        sent(q).wait()
    white_copy.wait()


def match(inside, lower, second, coef, bands):
    moved, part, mid, mid_slabs = inside
    rows, double, cols = moved.shape[1:]
    span = double // 2
    return pl.pallas_call(
        match_kernel,
        out_shape=(
            jax.ShapeDtypeStruct((span * rows, cols), BF16),
            jax.ShapeDtypeStruct((span * rows, cols), F32),
        ),
        in_specs=[vmem()] * 11,
        out_specs=(pl.BlockSpec(memory_space=pltpu.HBM),) * 2,
        scratch_shapes=[
            pltpu.VMEM((5, rows // 2, double, cols), F32),
            pltpu.VMEM((2, 32, cols), F32),
            pltpu.VMEM((4, double, cols), F32),
            pltpu.VMEM((6, 4, 5, double - 16, cols), BF16),
            pltpu.VMEM((span * rows, cols), F32),
            pltpu.VMEM((span * rows, cols), BF16),
            pltpu.VMEM((span * rows, cols), F32),
            pltpu.SemaphoreType.DMA((span // (4 * SHIFT) + 1,)),
        ],
        compiler_params=params(16),
        cost_estimate=pl.CostEstimate(flops=11 * 10**9, bytes_accessed=10**7, transcendentals=0),
        name="match",
    )(second, moved, part, mid, mid_slabs, *lower, coef, *bands)


def shards(raw_signal, fir_taps, white_coef, templates):
    span, rows, cols = raw_signal.shape
    raw = raw_signal.reshape(span * rows, cols)
    coef = white_coef.reshape(-1, cols)
    far, raw = opening(raw, rows, fir_taps.shape[0])
    far = swap_pairs(far, "tm", 1)
    near = swap_pairs(raw, "tm", 0)
    band, *bands, coef = prep(fir_taps, templates, coef, span, rows)
    filt, first, second = fir(band, raw, near, far, coef, rows)
    first = swap_pairs(first, "rows", 0)
    second = swap_pairs(second, "rows", 1)
    inside = inner(filt, coef)
    lower = after(first, inside, coef)
    whitened, best = match(inside, lower, second, coef, bands)
    return whitened.reshape(span, rows, cols), best.reshape(span, rows, cols)


def solution(mesh):
    return jax.shard_map(
        shards,
        mesh=mesh,
        in_specs=(P("tm", "rows", None), P(), P(None, "rows", None), P()),
        out_specs=(P("tm", "rows", None), P("tm", "rows", None)),
        check_vma=False,
    )
```

```python
import jax
import jax.numpy as jnp
from jax import lax
from jax.experimental import pallas as pl
from jax.experimental.pallas import tpu as pltpu
from jax.sharding import PartitionSpec as P


F32 = jnp.float32
BF16 = jnp.bfloat16
SHIFT = 4


def vmem():
    return pl.BlockSpec(memory_space=pltpu.VMEM)


def params(mib):
    return pltpu.CompilerParams(vmem_limit_bytes=mib * 1024 * 1024)


def swap_pairs(array, axis, first):
    size = lax.axis_size(axis)
    pairs = []
    for low in range(first, size - 1, 2):
        pairs += [(low, low + 1), (low + 1, low)]
    return lax.ppermute(array, axis, pairs)


def is_upper():
    return lax.rem(lax.axis_index("rows"), 2) == 0


def open_kernel(raw_ref, far_ref, keep_ref):
    skip = raw_ref.shape[0] - far_ref.shape[0]
    even = lax.rem(lax.axis_index("tm"), 2) == 0
    start = pl.multiple_of(jnp.where(even, 0, skip), 16)
    far_ref[...] = raw_ref[pl.ds(start, far_ref.shape[0]), :].astype(BF16)
    keep_ref[...] = raw_ref[...]


def opening(raw, rows, taps):
    return pl.pallas_call(
        open_kernel,
        out_shape=(
            jax.ShapeDtypeStruct(((taps - 1) * rows, raw.shape[1]), BF16),
            jax.ShapeDtypeStruct(raw.shape, F32),
        ),
        in_specs=[vmem()],
        out_specs=(vmem(), vmem()),
        compiler_params=params(4),
        cost_estimate=pl.CostEstimate(flops=10**5, bytes_accessed=10**6, transcendentals=0),
        name="opening",
    )(raw)


def prep_kernel(
    line_ref, tmpl_ref, coef_in_ref, band_ref, sum_ref, even_ref, odd_ref, coef_ref, wide, mixed
):
    _, count, length = tmpl_ref.shape
    own_rows = coef_ref.shape[0]
    upper = is_upper()
    for a in range(5):
        source = jnp.where(upper, a, 4 - a) * (5 * own_rows)
        for r in range(own_rows):
            line = pl.ds(source + jnp.where(upper, r, own_rows - 1 - r), 5, stride=own_rows)
            coef_ref[r, 5 * a : 5 * a + 5, :] = coef_in_ref[line, :]
    rows = band_ref.shape[0]
    line = jnp.broadcast_to(line_ref[...], (rows, 256))
    band = pltpu.roll(line, 0, 1, stride=1, stride_axis=0)
    high = band.astype(BF16)
    low = (band - high.astype(F32)).astype(BF16)
    band_ref[:, 0:256] = high
    band_ref[:, 256:512] = low
    band_ref[:, 512:768] = high

    wide[...] = jnp.zeros_like(wide)
    for a in range(5):
        source = jnp.where(upper, a, 4 - a) * 5
        for b in range(5):
            wide[5 * a + b, :, 0:length] = tmpl_ref[source + b].astype(F32)

    def even_spot(k):
        return wide[10 * (k // 5) + k % 5]

    def odd_spot(k):
        return wide[10 * (k // 5) + 5 + k % 5]

    def both_spots(k):
        return even_spot(k) + odd_spot(k) if k < 10 else even_spot(k)

    slot = 0
    for out_ref, piece, size in ((sum_ref, both_spots, 15), (even_ref, even_spot, 15), (odd_ref, odd_spot, 10)):
        for p in range(0, size, 2):
            pair = piece(p)
            if p + 1 < size:
                pair = pair + pltpu.roll(piece(p + 1), 64, 1)
            for b in range(SHIFT):
                moved = pltpu.roll(pair, b, 1) if b else pair
                mixed[slot, pl.ds(b, count, stride=SHIFT), :] = moved
            out_ref[:, 64 * p : 64 * p + 128] = mixed[slot].astype(BF16)
            slot += 1


def prep(fir_taps, templates, coef, span, rows):
    count, _, spots = templates.shape
    taps = fir_taps.shape[0]
    line = jnp.pad(fir_taps[::-1], (span - taps + 1, 255 - span))[None]
    by_spot = jnp.transpose(templates, (2, 0, 1))
    return pl.pallas_call(
        prep_kernel,
        out_shape=(
            jax.ShapeDtypeStruct((2 * span, 768), BF16),
            jax.ShapeDtypeStruct((count * SHIFT, 16 * 64), BF16),
            jax.ShapeDtypeStruct((count * SHIFT, 16 * 64), BF16),
            jax.ShapeDtypeStruct((count * SHIFT, 10 * 64), BF16),
            jax.ShapeDtypeStruct((rows, 32, coef.shape[1]), F32),
        ),
        in_specs=[vmem()] * 3,
        out_specs=(vmem(),) * 5,
        scratch_shapes=[
            pltpu.VMEM((spots, count, 128), F32),
            pltpu.VMEM((21, count * SHIFT, 128), F32),
        ],
        compiler_params=params(8),
        cost_estimate=pl.CostEstimate(flops=10**7, bytes_accessed=2 * 10**6, transcendentals=0),
        name="prep",
    )(line, by_spot, coef)


def fir_kernel(band_ref, raw_ref, near_ref, far_ref, coef_ref, filt_ref, first_ref, second_ref, widened, block):
    rows, double, cols = filt_ref.shape
    span = double // 2
    half = rows // 2
    even = lax.rem(lax.axis_index("tm"), 2) == 0
    short = far_ref.shape[0]
    skip = widened.shape[0] - short
    widened[0:skip, :] = jnp.zeros((skip, cols), F32)
    widened[short:, :] = jnp.zeros((skip, cols), F32)
    widened[pl.ds(pl.multiple_of(jnp.where(even, skip, 0), 16), short), :] = far_ref[...].astype(F32)
    columns = []
    upper = is_upper()
    for r in range(rows):
        line = pl.ds(jnp.where(upper, r, rows - 1 - r), span, stride=rows)
        near = near_ref[line, :]
        far = widened[line, :]
        own = raw_ref[line, :]
        before = jnp.where(even, far, near)
        after = jnp.where(even, near, far)
        line = jnp.concatenate([before, own, after, jnp.zeros_like(own)], axis=0)
        high = line.astype(BF16)
        low = (line - high.astype(F32)).astype(BF16)
        columns.append(jnp.concatenate([high, high, low], axis=0))
    for r in range(0, rows, 2):
        pair = jnp.concatenate(columns[r : r + 2], axis=1)
        out = jnp.dot(band_ref[...], pair, preferred_element_type=F32).astype(BF16)
        filt_ref[r] = out[:, :cols]
        filt_ref[r + 1] = out[:, cols:]
    base = half * double
    for side, order, edge in (
        (first_ref, range(rows - 1, rows - half - 1, -1), (rows - 1, rows - 2)),
        (second_ref, range(half - 1, -1, -1), (1, 0)),
    ):
        for k, r in enumerate(order):
            side[double * k : double * (k + 1), :] = filt_ref[r]
        for k, r in enumerate(edge):
            block[...] = jnp.zeros_like(block)
            for a in range(5):
                block[5 * a : 5 * a + 5, :] = coef_ref[r, 20 - 5 * a : 25 - 5 * a, :]
            side[base + 32 * k : base + 32 * k + 32, :] = block[...].astype(BF16)


def fir(band, raw, near, far, coef, rows):
    span = raw.shape[0] // rows
    cols = raw.shape[1]
    message = jax.ShapeDtypeStruct((rows // 2 * 2 * span + 64, cols), BF16)
    return pl.pallas_call(
        fir_kernel,
        out_shape=(jax.ShapeDtypeStruct((rows, 2 * span, cols), BF16), message, message),
        in_specs=[vmem()] * 5,
        out_specs=(vmem(),) * 3,
        scratch_shapes=[pltpu.VMEM(raw.shape, F32), pltpu.VMEM(coef.shape[1:], F32)],
        compiler_params=params(8),
        cost_estimate=pl.CostEstimate(flops=2 * 10**8, bytes_accessed=2 * 10**6, transcendentals=0),
        name="fir",
    )(band, raw, near, far, coef)


def shifter(shape):
    cols = shape[1]
    lane = lax.broadcasted_iota(jnp.int32, shape, 1)

    def shifted(x, b):
        if b == 2:
            return x
        out = pltpu.roll(x, (2 - b) % cols, 1)
        valid = lane >= 2 - b if b < 2 else lane < cols + 2 - b
        return jnp.where(valid, out, 0.0)

    return shifted


def closer(shape):
    span = shape[0] // 2
    last = lax.axis_index("tm") == lax.axis_size("tm") - 1
    time = lax.broadcasted_iota(jnp.int32, shape, 0)
    keep = jnp.logical_not(jnp.logical_and(last, time >= span))

    def closed(x):
        return jnp.where(keep, x, 0.0).astype(BF16).astype(F32)

    return closed


def build_slab(slab, x, shifted):
    double = x.shape[0]
    for b in range(5):
        moved = shifted(x, b)
        later = pltpu.roll(moved, double - SHIFT, 0)
        for f in range(4):
            piece = (later if f % 2 else moved)[8 * (f // 2) : 8 * (f // 2) + double - 16]
            slab[f, b] = piece.astype(BF16)


def inner_kernel(filt_ref, coef_ref, moved_ref, part_ref, white_ref, slab_ref):
    rows, double, cols = filt_ref.shape
    shifted = shifter((double, cols))
    closed = closer((double, cols))

    def spread(r, _):
        x = filt_ref[r].astype(F32)
        for b in range(5):
            moved_ref[b, r] = shifted(x, b)
        return 0

    lax.fori_loop(0, rows, spread, 0)

    def sums(r):
        total = jnp.zeros((double, cols), F32)
        for a in range(5):
            if 0 <= r + a - 2 < rows:
                for b in range(5):
                    s = 5 * a + b
                    total = total + coef_ref[r, s : s + 1, :] * moved_ref[b, r + a - 2]
        return total

    for k, r in enumerate((0, 1, rows - 2, rows - 1)):
        part_ref[k] = sums(r)
    for r in range(2, rows - 2):
        white_ref[r - 2] = closed(sums(r))
    build_slab(slab_ref.at[0], white_ref[1], shifted)
    build_slab(slab_ref.at[1], white_ref[3], shifted)
    build_slab(slab_ref.at[2], white_ref[0] - white_ref[1], shifted)
    build_slab(slab_ref.at[3], white_ref[2] - white_ref[3], shifted)
    build_slab(slab_ref.at[4], white_ref[2] - white_ref[1], shifted)


def inner(filt, coef):
    rows, double, cols = filt.shape
    return pl.pallas_call(
        inner_kernel,
        out_shape=(
            jax.ShapeDtypeStruct((5, rows, double, cols), F32),
            jax.ShapeDtypeStruct((4, double, cols), F32),
            jax.ShapeDtypeStruct((rows - 4, double, cols), F32),
            jax.ShapeDtypeStruct((5, 4, 5, double - 16, cols), BF16),
        ),
        in_specs=[vmem()] * 2,
        out_specs=(vmem(),) * 4,
        compiler_params=params(12),
        cost_estimate=pl.CostEstimate(flops=10**9, bytes_accessed=10**7, transcendentals=0),
        name="inner",
    )(filt, coef)


def spread_halo(side, halo, edge, shifted):
    half, double = halo.shape[1:3]

    def spread(k, _):
        x = side[pl.ds(pl.multiple_of(k * double, double), double), :].astype(F32)
        for b in range(5):
            halo[b, k] = shifted(x, b)
        return 0

    lax.fori_loop(0, half, spread, 0)
    base = half * double
    for k in range(2):
        edge[k] = side[base + 32 * k : base + 32 * k + 32, :].astype(F32)


def gather(total, weights, lines):
    for s, piece in lines:
        total = total + weights[s : s + 1, :] * piece
    return total


def score_block(lhs, plain, level, step, f, start):
    def product(lhs_ref, source, depth):
        cols = source[0].shape[-1]
        blank = [jnp.zeros((64, cols), BF16)] * (depth % 2)
        columns = [
            jnp.concatenate(
                [source[m + j][f, b, pl.ds(start, 64), :] for j in range(depth) for b in range(5)] + blank, axis=0
            )
            for m in range(2)
        ]
        found = jnp.dot(lhs_ref[...], jnp.concatenate(columns, axis=1), preferred_element_type=F32)
        return found.reshape(found.shape[0] // 8, 8, 2 * cols)

    def top(found):
        high = jnp.max(found, axis=0)
        return jnp.maximum(high, pltpu.roll(high, 4, 0))

    sum_ref, even_ref, odd_ref = lhs
    shared = product(sum_ref, plain, 3)
    return top(product(even_ref, level, 3) + shared), top(product(odd_ref, step, 2) + shared)


def after_kernel(
    side_ref,
    moved_ref,
    part_ref,
    mid_ref,
    mid_slab_ref,
    coef_ref,
    sum_ref,
    even_ref,
    odd_ref,
    white_ref,
    half_ref,
    slab_ref,
    halo,
    edge,
    white,
):
    rows, double, cols = moved_ref.shape[1:]
    half = rows // 2
    shifted = shifter((double, cols))
    closed = closer((double, cols))
    spread_halo(side_ref, halo, edge, shifted)

    def lines(w, offsets):
        for a in offsets:
            row = w + a - half
            for b in range(5):
                yield 5 * a + b, moved_ref[b, row] if row < rows else halo[b, row - rows]

    zero = jnp.zeros((double, cols), F32)
    white[0] = closed(gather(part_ref[2], coef_ref.at[rows - 2], lines(rows, (4,))))
    white[1] = closed(gather(part_ref[3], coef_ref.at[rows - 1], lines(rows + 1, (3, 4))))
    white[2] = closed(gather(zero, edge.at[0], lines(rows + 2, range(5))))
    white[3] = closed(gather(zero, edge.at[1], lines(rows + 3, range(5))))
    white_ref[0] = white[0, 0 : double // 2]
    white_ref[1] = white[1, 0 : double // 2]
    build_slab(slab_ref.at[0], white[1], shifted)
    build_slab(slab_ref.at[1], white[3], shifted)
    build_slab(slab_ref.at[2], white[0] - white[1], shifted)
    build_slab(slab_ref.at[3], white[2] - white[3], shifted)
    build_slab(slab_ref.at[4], white[0] - mid_ref[rows - 5], shifted)
    build_slab(slab_ref.at[5], white[2] - white[1], shifted)

    low = [slab_ref.at[k] for k in range(6)]
    mids = [mid_slab_ref.at[k] for k in range(5)]
    plain, level, step = mids[0:2] + low[0:2], mids[2:4] + low[2:4], mids[4:5] + low[4:6]

    def score(q, _):
        start = pl.multiple_of(q * 16, 16)
        for f in range(4):
            found = score_block((sum_ref, even_ref, odd_ref), plain, level, step, f, start)
            for r in range(half):
                first_row = (q * 4 + f) * SHIFT * half + r
                piece = found[r % 2][0:SHIFT, cols * (r // 2) : cols * (r // 2 + 1)]
                half_ref[pl.ds(first_row, SHIFT, stride=half), :] = piece
        return 0

    lax.fori_loop(0, double // 2 // (4 * SHIFT), score, 0, unroll=True)


def after(side, inside, coef, bands):
    moved, part, mid, mid_slabs = inside
    rows, double, cols = moved.shape[1:]
    return pl.pallas_call(
        after_kernel,
        out_shape=(
            jax.ShapeDtypeStruct((2, double // 2, cols), F32),
            jax.ShapeDtypeStruct((double // 2 * rows // 2, cols), F32),
        ),
        in_specs=[vmem()] * 9,
        out_specs=(vmem(),) * 2,
        scratch_shapes=[
            pltpu.VMEM((6, 4, 5, double - 16, cols), BF16),
            pltpu.VMEM((5, rows // 2, double, cols), F32),
            pltpu.VMEM((2, 32, cols), F32),
            pltpu.VMEM((4, double, cols), F32),
        ],
        compiler_params=params(16),
        cost_estimate=pl.CostEstimate(flops=6 * 10**9, bytes_accessed=10**7, transcendentals=0),
        name="after",
    )(side, moved, part, mid, mid_slabs, coef, *bands)


def match_kernel(
    side_ref,
    moved_ref,
    part_ref,
    mid_ref,
    mid_slab_ref,
    low_ref,
    half_ref,
    coef_ref,
    sum_ref,
    even_ref,
    odd_ref,
    white_hbm,
    best_hbm,
    halo,
    edge,
    white,
    slabs,
    natural,
    rounded,
    best,
    sems,
):
    rows, double, cols = moved_ref.shape[1:]
    span = double // 2
    half = rows // 2
    shifted = shifter((double, cols))
    closed = closer((double, cols))
    upper = is_upper()

    def actual(r):
        return jnp.where(upper, r, rows - 1 - r)

    spread_halo(side_ref, halo, edge, shifted)

    def lines(w, offsets):
        for a in offsets:
            row = w + a
            for b in range(5):
                yield 5 * a + b, halo[b, row] if row < half else moved_ref[b, row - half]

    zero = jnp.zeros((double, cols), F32)
    white[0] = closed(gather(zero, edge.at[0], lines(0, range(5))))
    white[1] = closed(gather(zero, edge.at[1], lines(1, range(5))))
    white[2] = closed(gather(part_ref[0], coef_ref.at[0], lines(2, (0, 1))))
    white[3] = closed(gather(part_ref[1], coef_ref.at[1], lines(3, (0,))))
    for r in range(rows):
        if r < 2:
            line = white[r + 2, 0:span]
        elif r < rows - 2:
            line = mid_ref[r - 2, 0:span]
        else:
            line = low_ref[r - rows + 2]
        natural[pl.ds(actual(r), span, stride=rows), :] = line
    rounded[...] = natural[...].astype(BF16)
    white_copy = pltpu.make_async_copy(rounded, white_hbm, sems.at[span // (4 * SHIFT)])
    white_copy.start()

    build_slab(slabs.at[0], white[1], shifted)
    build_slab(slabs.at[1], white[3], shifted)
    build_slab(slabs.at[2], white[0] - white[1], shifted)
    build_slab(slabs.at[3], white[2] - white[3], shifted)
    build_slab(slabs.at[4], white[2] - white[1], shifted)
    build_slab(slabs.at[5], mid_ref[0] - white[3], shifted)
    for r in range(half):
        best[pl.ds(actual(half + r), span, stride=rows), :] = half_ref[pl.ds(r, span, stride=half), :]
    high = [slabs.at[k] for k in range(6)]
    mids = [mid_slab_ref.at[k] for k in range(5)]
    plain, level, step = high[0:2] + mids[0:2], high[2:4] + mids[2:4], high[4:6] + mids[4:5]

    chunk = 4 * SHIFT * rows

    def sent(q):
        part = pl.ds(pl.multiple_of(q * chunk, chunk), chunk)
        return pltpu.make_async_copy(best.at[part, :], best_hbm.at[part, :], sems.at[q])

    def score(q, _):
        start = pl.multiple_of(q * 16, 16)
        for f in range(4):
            found = score_block((sum_ref, even_ref, odd_ref), plain, level, step, f, start)
            for r in range(half):
                first_row = q * chunk + SHIFT * rows * f + actual(r)
                piece = found[r % 2][0:SHIFT, cols * (r // 2) : cols * (r // 2 + 1)]
                best[pl.ds(first_row, SHIFT, stride=rows), :] = piece
        sent(q).start()
        return 0

    parts = span // (4 * SHIFT)
    lax.fori_loop(0, parts, score, 0, unroll=True)
    for q in range(parts):
        sent(q).wait()
    white_copy.wait()


def match(inside, lower, second, coef, bands):
    moved, part, mid, mid_slabs = inside
    rows, double, cols = moved.shape[1:]
    span = double // 2
    return pl.pallas_call(
        match_kernel,
        out_shape=(
            jax.ShapeDtypeStruct((span * rows, cols), BF16),
            jax.ShapeDtypeStruct((span * rows, cols), F32),
        ),
        in_specs=[vmem()] * 11,
        out_specs=(pl.BlockSpec(memory_space=pltpu.HBM),) * 2,
        scratch_shapes=[
            pltpu.VMEM((5, rows // 2, double, cols), F32),
            pltpu.VMEM((2, 32, cols), F32),
            pltpu.VMEM((4, double, cols), F32),
            pltpu.VMEM((6, 4, 5, double - 16, cols), BF16),
            pltpu.VMEM((span * rows, cols), F32),
            pltpu.VMEM((span * rows, cols), BF16),
            pltpu.VMEM((span * rows, cols), F32),
            pltpu.SemaphoreType.DMA((span // (4 * SHIFT) + 1,)),
        ],
        compiler_params=params(16),
        cost_estimate=pl.CostEstimate(flops=6 * 10**9, bytes_accessed=10**7, transcendentals=0),
        name="match",
    )(second, moved, part, mid, mid_slabs, *lower, coef, *bands)


def shards(raw_signal, fir_taps, white_coef, templates):
    span, rows, cols = raw_signal.shape
    raw = raw_signal.reshape(span * rows, cols)
    coef = white_coef.reshape(-1, cols)
    far, raw = opening(raw, rows, fir_taps.shape[0])
    far = swap_pairs(far, "tm", 1)
    near = swap_pairs(raw, "tm", 0)
    band, *bands, coef = prep(fir_taps, templates, coef, span, rows)
    filt, first, second = fir(band, raw, near, far, coef, rows)
    first = swap_pairs(first, "rows", 0)
    second = swap_pairs(second, "rows", 1)
    inside = inner(filt, coef)
    lower = after(first, inside, coef, bands)
    whitened, best = match(inside, lower, second, coef, bands)
    return whitened.reshape(span, rows, cols), best.reshape(span, rows, cols)


def solution(mesh):
    return jax.shard_map(
        shards,
        mesh=mesh,
        in_specs=(P("tm", "rows", None), P(), P(None, "rows", None), P()),
        out_specs=(P("tm", "rows", None), P("tm", "rows", None)),
        check_vma=False,
    )
```

```python
import jax
import jax.numpy as jnp
from jax import lax
from jax.experimental import pallas as pl
from jax.experimental.pallas import tpu as pltpu
from jax.sharding import PartitionSpec as P


F32 = jnp.float32
BF16 = jnp.bfloat16
SHIFT = 4


def vmem():
    return pl.BlockSpec(memory_space=pltpu.VMEM)


def params(mib):
    return pltpu.CompilerParams(vmem_limit_bytes=mib * 1024 * 1024)


def swap_pairs(array, axis, first):
    size = lax.axis_size(axis)
    pairs = []
    for low in range(first, size - 1, 2):
        pairs += [(low, low + 1), (low + 1, low)]
    return lax.ppermute(array, axis, pairs)


def is_upper():
    return lax.rem(lax.axis_index("rows"), 2) == 0


def open_kernel(raw_ref, far_ref, keep_ref):
    skip = raw_ref.shape[0] - far_ref.shape[0]
    even = lax.rem(lax.axis_index("tm"), 2) == 0
    start = pl.multiple_of(jnp.where(even, 0, skip), 16)
    far_ref[...] = raw_ref[pl.ds(start, far_ref.shape[0]), :].astype(BF16)
    keep_ref[...] = raw_ref[...]


def opening(raw, rows, taps):
    return pl.pallas_call(
        open_kernel,
        out_shape=(
            jax.ShapeDtypeStruct(((taps - 1) * rows, raw.shape[1]), BF16),
            jax.ShapeDtypeStruct(raw.shape, F32),
        ),
        in_specs=[vmem()],
        out_specs=(vmem(), vmem()),
        compiler_params=params(4),
        cost_estimate=pl.CostEstimate(flops=10**5, bytes_accessed=10**6, transcendentals=0),
        name="opening",
    )(raw)


def prep_kernel(
    line_ref, tmpl_ref, coef_in_ref, band_ref, sum_ref, even_ref, odd_ref, coef_ref, wide, mixed
):
    _, count, length = tmpl_ref.shape
    own_rows = coef_ref.shape[0]
    upper = is_upper()
    for a in range(5):
        source = jnp.where(upper, a, 4 - a) * (5 * own_rows)
        for r in range(own_rows):
            line = pl.ds(source + jnp.where(upper, r, own_rows - 1 - r), 5, stride=own_rows)
            coef_ref[r, 5 * a : 5 * a + 5, :] = coef_in_ref[line, :]
    rows = band_ref.shape[0]
    line = jnp.broadcast_to(line_ref[...], (rows, 256))
    band = pltpu.roll(line, 0, 1, stride=1, stride_axis=0)
    high = band.astype(BF16)
    low = (band - high.astype(F32)).astype(BF16)
    band_ref[:, 0:256] = high
    band_ref[:, 256:512] = low
    band_ref[:, 512:768] = high

    wide[...] = jnp.zeros_like(wide)
    for a in range(5):
        source = jnp.where(upper, a, 4 - a) * 5
        for b in range(5):
            wide[5 * a + b, :, 0:length] = tmpl_ref[source + b].astype(F32)

    def even_spot(k):
        return wide[10 * (k // 5) + k % 5]

    def odd_spot(k):
        return wide[10 * (k // 5) + 5 + k % 5]

    def both_spots(k):
        return even_spot(k) + odd_spot(k) if k < 10 else even_spot(k)

    slot = 0
    for out_ref, piece, size in ((sum_ref, both_spots, 15), (even_ref, even_spot, 15), (odd_ref, odd_spot, 10)):
        for p in range(0, size, 2):
            pair = piece(p)
            if p + 1 < size:
                pair = pair + pltpu.roll(piece(p + 1), 64, 1)
            for b in range(SHIFT):
                moved = pltpu.roll(pair, b, 1) if b else pair
                mixed[slot, pl.ds(b, count, stride=SHIFT), :] = moved
            out_ref[:, 64 * p : 64 * p + 128] = mixed[slot].astype(BF16)
            slot += 1


def prep(fir_taps, templates, coef, span, rows):
    count, _, spots = templates.shape
    taps = fir_taps.shape[0]
    line = jnp.pad(fir_taps[::-1], (span - taps + 1, 255 - span))[None]
    by_spot = jnp.transpose(templates, (2, 0, 1))
    return pl.pallas_call(
        prep_kernel,
        out_shape=(
            jax.ShapeDtypeStruct((2 * span, 768), BF16),
            jax.ShapeDtypeStruct((count * SHIFT, 16 * 64), BF16),
            jax.ShapeDtypeStruct((count * SHIFT, 16 * 64), BF16),
            jax.ShapeDtypeStruct((count * SHIFT, 10 * 64), BF16),
            jax.ShapeDtypeStruct((rows, 32, coef.shape[1]), F32),
        ),
        in_specs=[vmem()] * 3,
        out_specs=(vmem(),) * 5,
        scratch_shapes=[
            pltpu.VMEM((spots, count, 128), F32),
            pltpu.VMEM((21, count * SHIFT, 128), F32),
        ],
        compiler_params=params(8),
        cost_estimate=pl.CostEstimate(flops=10**7, bytes_accessed=2 * 10**6, transcendentals=0),
        name="prep",
    )(line, by_spot, coef)


def fir_kernel(band_ref, raw_ref, near_ref, far_ref, coef_ref, filt_ref, first_ref, second_ref, widened, block):
    rows, double, cols = filt_ref.shape
    span = double // 2
    half = rows // 2
    even = lax.rem(lax.axis_index("tm"), 2) == 0
    short = far_ref.shape[0]
    skip = widened.shape[0] - short
    widened[0:skip, :] = jnp.zeros((skip, cols), F32)
    widened[short:, :] = jnp.zeros((skip, cols), F32)
    widened[pl.ds(pl.multiple_of(jnp.where(even, skip, 0), 16), short), :] = far_ref[...].astype(F32)
    columns = []
    upper = is_upper()
    for r in range(rows):
        line = pl.ds(jnp.where(upper, r, rows - 1 - r), span, stride=rows)
        near = near_ref[line, :]
        far = widened[line, :]
        own = raw_ref[line, :]
        before = jnp.where(even, far, near)
        after = jnp.where(even, near, far)
        line = jnp.concatenate([before, own, after, jnp.zeros_like(own)], axis=0)
        high = line.astype(BF16)
        low = (line - high.astype(F32)).astype(BF16)
        columns.append(jnp.concatenate([high, high, low], axis=0))
    for r in range(0, rows, 2):
        pair = jnp.concatenate(columns[r : r + 2], axis=1)
        out = jnp.dot(band_ref[...], pair, preferred_element_type=F32).astype(BF16)
        filt_ref[r] = out[:, :cols]
        filt_ref[r + 1] = out[:, cols:]
    base = half * double
    for side, order, edge in (
        (first_ref, range(rows - 1, rows - half - 1, -1), (rows - 1, rows - 2)),
        (second_ref, range(half - 1, -1, -1), (1, 0)),
    ):
        for k, r in enumerate(order):
            side[double * k : double * (k + 1), :] = filt_ref[r]
        for k, r in enumerate(edge):
            block[...] = jnp.zeros_like(block)
            for a in range(5):
                block[5 * a : 5 * a + 5, :] = coef_ref[r, 20 - 5 * a : 25 - 5 * a, :]
            side[base + 32 * k : base + 32 * k + 32, :] = block[...].astype(BF16)


def fir(band, raw, near, far, coef, rows):
    span = raw.shape[0] // rows
    cols = raw.shape[1]
    message = jax.ShapeDtypeStruct((rows // 2 * 2 * span + 64, cols), BF16)
    return pl.pallas_call(
        fir_kernel,
        out_shape=(jax.ShapeDtypeStruct((rows, 2 * span, cols), BF16), message, message),
        in_specs=[vmem()] * 5,
        out_specs=(vmem(),) * 3,
        scratch_shapes=[pltpu.VMEM(raw.shape, F32), pltpu.VMEM(coef.shape[1:], F32)],
        compiler_params=params(8),
        cost_estimate=pl.CostEstimate(flops=2 * 10**8, bytes_accessed=2 * 10**6, transcendentals=0),
        name="fir",
    )(band, raw, near, far, coef)


def shifter(shape):
    cols = shape[1]
    lane = lax.broadcasted_iota(jnp.int32, shape, 1)

    def shifted(x, b):
        if b == 2:
            return x
        out = pltpu.roll(x, (2 - b) % cols, 1)
        valid = lane >= 2 - b if b < 2 else lane < cols + 2 - b
        return jnp.where(valid, out, 0.0)

    return shifted


def closer(shape):
    span = shape[0] // 2
    last = lax.axis_index("tm") == lax.axis_size("tm") - 1
    time = lax.broadcasted_iota(jnp.int32, shape, 0)
    keep = jnp.logical_not(jnp.logical_and(last, time >= span))

    def closed(x):
        return jnp.where(keep, x, 0.0).astype(BF16).astype(F32)

    return closed


def build_slab(slab, x, shifted):
    double = x.shape[0]
    for b in range(5):
        moved = shifted(x, b)
        later = pltpu.roll(moved, double - SHIFT, 0)
        for f in range(4):
            piece = (later if f % 2 else moved)[8 * (f // 2) : 8 * (f // 2) + double - 16]
            slab[f, b] = piece.astype(BF16)


def inner_kernel(filt_ref, coef_ref, moved_ref, part_ref, white_ref, slab_ref):
    rows, double, cols = filt_ref.shape
    shifted = shifter((double, cols))
    closed = closer((double, cols))

    def spread(r, _):
        x = filt_ref[r].astype(F32)
        for b in range(5):
            moved_ref[b, r] = shifted(x, b)
        return 0

    lax.fori_loop(0, rows, spread, 0)

    def sums(r):
        total = jnp.zeros((double, cols), F32)
        for a in range(5):
            if 0 <= r + a - 2 < rows:
                for b in range(5):
                    s = 5 * a + b
                    total = total + coef_ref[r, s : s + 1, :] * moved_ref[b, r + a - 2]
        return total

    for k, r in enumerate((0, 1, rows - 2, rows - 1)):
        part_ref[k] = sums(r)
    for r in range(2, rows - 2):
        white_ref[r - 2] = closed(sums(r))
    build_slab(slab_ref.at[0], white_ref[1], shifted)
    build_slab(slab_ref.at[1], white_ref[3], shifted)
    build_slab(slab_ref.at[2], white_ref[0] - white_ref[1], shifted)
    build_slab(slab_ref.at[3], white_ref[2] - white_ref[3], shifted)
    build_slab(slab_ref.at[4], white_ref[2] - white_ref[1], shifted)


def inner(filt, coef):
    rows, double, cols = filt.shape
    return pl.pallas_call(
        inner_kernel,
        out_shape=(
            jax.ShapeDtypeStruct((5, rows, double, cols), F32),
            jax.ShapeDtypeStruct((4, double, cols), F32),
            jax.ShapeDtypeStruct((rows - 4, double, cols), F32),
            jax.ShapeDtypeStruct((5, 4, 5, double - 16, cols), BF16),
        ),
        in_specs=[vmem()] * 2,
        out_specs=(vmem(),) * 4,
        compiler_params=params(12),
        cost_estimate=pl.CostEstimate(flops=10**9, bytes_accessed=10**7, transcendentals=0),
        name="inner",
    )(filt, coef)


def spread_halo(side, halo, edge, shifted):
    half, double = halo.shape[1:3]

    def spread(k, _):
        x = side[pl.ds(pl.multiple_of(k * double, double), double), :].astype(F32)
        for b in range(5):
            halo[b, k] = shifted(x, b)
        return 0

    lax.fori_loop(0, half, spread, 0, unroll=True)
    base = half * double
    for k in range(2):
        edge[k] = side[base + 32 * k : base + 32 * k + 32, :].astype(F32)


def gather(total, weights, lines):
    for s, piece in lines:
        total = total + weights[s : s + 1, :] * piece
    return total


def score_block(lhs, plain, level, step, f, start):
    def product(lhs_ref, source, depth):
        cols = source[0].shape[-1]
        blank = [jnp.zeros((64, cols), BF16)] * (depth % 2)
        columns = [
            jnp.concatenate(
                [source[m + j][f, b, pl.ds(start, 64), :] for j in range(depth) for b in range(5)] + blank, axis=0
            )
            for m in range(2)
        ]
        found = jnp.dot(lhs_ref[...], jnp.concatenate(columns, axis=1), preferred_element_type=F32)
        return found.reshape(found.shape[0] // 8, 8, 2 * cols)

    def top(found):
        high = jnp.max(found, axis=0)
        return jnp.maximum(high, pltpu.roll(high, 4, 0))

    sum_ref, even_ref, odd_ref = lhs
    shared = product(sum_ref, plain, 3)
    return top(product(even_ref, level, 3) + shared), top(product(odd_ref, step, 2) + shared)


def after_kernel(
    side_ref,
    moved_ref,
    part_ref,
    mid_ref,
    mid_slab_ref,
    coef_ref,
    sum_ref,
    even_ref,
    odd_ref,
    white_ref,
    half_ref,
    slab_ref,
    halo,
    edge,
    white,
):
    rows, double, cols = moved_ref.shape[1:]
    half = rows // 2
    shifted = shifter((double, cols))
    closed = closer((double, cols))
    spread_halo(side_ref, halo, edge, shifted)

    def lines(w, offsets):
        for a in offsets:
            row = w + a - half
            for b in range(5):
                yield 5 * a + b, moved_ref[b, row] if row < rows else halo[b, row - rows]

    zero = jnp.zeros((double, cols), F32)
    white[0] = closed(gather(part_ref[2], coef_ref.at[rows - 2], lines(rows, (4,))))
    white[1] = closed(gather(part_ref[3], coef_ref.at[rows - 1], lines(rows + 1, (3, 4))))
    white[2] = closed(gather(zero, edge.at[0], lines(rows + 2, range(5))))
    white[3] = closed(gather(zero, edge.at[1], lines(rows + 3, range(5))))
    white_ref[0] = white[0, 0 : double // 2]
    white_ref[1] = white[1, 0 : double // 2]
    build_slab(slab_ref.at[0], white[1], shifted)
    build_slab(slab_ref.at[1], white[3], shifted)
    build_slab(slab_ref.at[2], white[0] - white[1], shifted)
    build_slab(slab_ref.at[3], white[2] - white[3], shifted)
    build_slab(slab_ref.at[4], white[0] - mid_ref[rows - 5], shifted)
    build_slab(slab_ref.at[5], white[2] - white[1], shifted)

    low = [slab_ref.at[k] for k in range(6)]
    mids = [mid_slab_ref.at[k] for k in range(5)]
    plain, level, step = mids[0:2] + low[0:2], mids[2:4] + low[2:4], mids[4:5] + low[4:6]

    def score(q, _):
        start = pl.multiple_of(q * 16, 16)
        for f in range(4):
            found = score_block((sum_ref, even_ref, odd_ref), plain, level, step, f, start)
            for r in range(half):
                first_row = (q * 4 + f) * SHIFT * half + r
                piece = found[r % 2][0:SHIFT, cols * (r // 2) : cols * (r // 2 + 1)]
                half_ref[pl.ds(first_row, SHIFT, stride=half), :] = piece
        return 0

    lax.fori_loop(0, double // 2 // (8 * SHIFT), score, 0, unroll=True)


def after(side, inside, coef, bands):
    moved, part, mid, mid_slabs = inside
    rows, double, cols = moved.shape[1:]
    return pl.pallas_call(
        after_kernel,
        out_shape=(
            jax.ShapeDtypeStruct((2, double // 2, cols), F32),
            jax.ShapeDtypeStruct((double // 4 * rows // 2, cols), F32),
            jax.ShapeDtypeStruct((6, 4, 5, double - 16, cols), BF16),
        ),
        in_specs=[vmem()] * 9,
        out_specs=(vmem(),) * 3,
        scratch_shapes=[
            pltpu.VMEM((5, rows // 2, double, cols), F32),
            pltpu.VMEM((2, 32, cols), F32),
            pltpu.VMEM((4, double, cols), F32),
        ],
        compiler_params=params(16),
        cost_estimate=pl.CostEstimate(flops=6 * 10**9, bytes_accessed=10**7, transcendentals=0),
        name="after",
    )(side, moved, part, mid, mid_slabs, coef, *bands)


def match_kernel(
    side_ref,
    moved_ref,
    part_ref,
    mid_ref,
    mid_slab_ref,
    low_ref,
    half_ref,
    low_slab_ref,
    coef_ref,
    sum_ref,
    even_ref,
    odd_ref,
    white_hbm,
    best_hbm,
    halo,
    edge,
    white,
    slabs,
    natural,
    rounded,
    best,
    sems,
):
    rows, double, cols = moved_ref.shape[1:]
    span = double // 2
    half = rows // 2
    shifted = shifter((double, cols))
    closed = closer((double, cols))
    upper = is_upper()

    def actual(r):
        return jnp.where(upper, r, rows - 1 - r)

    chunk = 4 * SHIFT * rows
    parts = span // (4 * SHIFT)
    lhs = (sum_ref, even_ref, odd_ref)
    mids = [mid_slab_ref.at[k] for k in range(5)]
    low = [low_slab_ref.at[k] for k in range(6)]

    def place(found, q, f, offset):
        for r in range(half):
            first_row = q * chunk + SHIFT * rows * f + actual(offset + r)
            piece = found[r % 2][0:SHIFT, cols * (r // 2) : cols * (r // 2 + 1)]
            best[pl.ds(first_row, SHIFT, stride=rows), :] = piece

    spread_halo(side_ref, halo, edge, shifted)
    for q in range(parts // 2, parts):
        for f in range(4):
            found = score_block(lhs, mids[0:2] + low[0:2], mids[2:4] + low[2:4], mids[4:5] + low[4:6], f, 16 * q)
            place(found, q, f, half)

    def lines(w, offsets):
        for a in offsets:
            row = w + a
            for b in range(5):
                yield 5 * a + b, halo[b, row] if row < half else moved_ref[b, row - half]

    zero = jnp.zeros((double, cols), F32)
    white[0] = closed(gather(zero, edge.at[0], lines(0, range(5))))
    white[1] = closed(gather(zero, edge.at[1], lines(1, range(5))))
    white[2] = closed(gather(part_ref[0], coef_ref.at[0], lines(2, (0, 1))))
    white[3] = closed(gather(part_ref[1], coef_ref.at[1], lines(3, (0,))))
    for r in range(rows):
        if r < 2:
            line = white[r + 2, 0:span]
        elif r < rows - 2:
            line = mid_ref[r - 2, 0:span]
        else:
            line = low_ref[r - rows + 2]
        natural[pl.ds(actual(r), span, stride=rows), :] = line
    rounded[...] = natural[...].astype(BF16)
    white_copy = pltpu.make_async_copy(rounded, white_hbm, sems.at[span // (4 * SHIFT)])
    white_copy.start()

    build_slab(slabs.at[0], white[1], shifted)
    build_slab(slabs.at[1], white[3], shifted)
    build_slab(slabs.at[2], white[0] - white[1], shifted)
    build_slab(slabs.at[3], white[2] - white[3], shifted)
    build_slab(slabs.at[4], white[2] - white[1], shifted)
    build_slab(slabs.at[5], mid_ref[0] - white[3], shifted)
    for r in range(half):
        best[pl.ds(actual(half + r), span // 2, stride=rows), :] = half_ref[pl.ds(r, span // 2, stride=half), :]
    high = [slabs.at[k] for k in range(6)]
    plain, level, step = high[0:2] + mids[0:2], high[2:4] + mids[2:4], high[4:6] + mids[4:5]

    def sent(q):
        part = pl.ds(pl.multiple_of(q * chunk, chunk), chunk)
        return pltpu.make_async_copy(best.at[part, :], best_hbm.at[part, :], sems.at[q])

    def score(q, _):
        start = pl.multiple_of(q * 16, 16)
        for f in range(4):
            place(score_block(lhs, plain, level, step, f, start), q, f, 0)
        sent(q).start()
        return 0

    lax.fori_loop(0, parts, score, 0, unroll=True)
    for q in range(parts):
        sent(q).wait()
    white_copy.wait()


def match(inside, lower, second, coef, bands):
    moved, part, mid, mid_slabs = inside
    rows, double, cols = moved.shape[1:]
    span = double // 2
    return pl.pallas_call(
        match_kernel,
        out_shape=(
            jax.ShapeDtypeStruct((span * rows, cols), BF16),
            jax.ShapeDtypeStruct((span * rows, cols), F32),
        ),
        in_specs=[vmem()] * 12,
        out_specs=(pl.BlockSpec(memory_space=pltpu.HBM),) * 2,
        scratch_shapes=[
            pltpu.VMEM((5, rows // 2, double, cols), F32),
            pltpu.VMEM((2, 32, cols), F32),
            pltpu.VMEM((4, double, cols), F32),
            pltpu.VMEM((6, 4, 5, double - 16, cols), BF16),
            pltpu.VMEM((span * rows, cols), F32),
            pltpu.VMEM((span * rows, cols), BF16),
            pltpu.VMEM((span * rows, cols), F32),
            pltpu.SemaphoreType.DMA((span // (4 * SHIFT) + 1,)),
        ],
        compiler_params=params(16),
        cost_estimate=pl.CostEstimate(flops=6 * 10**9, bytes_accessed=10**7, transcendentals=0),
        name="match",
    )(second, moved, part, mid, mid_slabs, *lower, coef, *bands)


def shards(raw_signal, fir_taps, white_coef, templates):
    span, rows, cols = raw_signal.shape
    raw = raw_signal.reshape(span * rows, cols)
    coef = white_coef.reshape(-1, cols)
    far, raw = opening(raw, rows, fir_taps.shape[0])
    far = swap_pairs(far, "tm", 1)
    near = swap_pairs(raw, "tm", 0)
    band, *bands, coef = prep(fir_taps, templates, coef, span, rows)
    filt, first, second = fir(band, raw, near, far, coef, rows)
    first = swap_pairs(first, "rows", 0)
    second = swap_pairs(second, "rows", 1)
    inside = inner(filt, coef)
    lower = after(first, inside, coef, bands)
    whitened, best = match(inside, lower, second, coef, bands)
    return whitened.reshape(span, rows, cols), best.reshape(span, rows, cols)


def solution(mesh):
    return jax.shard_map(
        shards,
        mesh=mesh,
        in_specs=(P("tm", "rows", None), P(), P(None, "rows", None), P()),
        out_specs=(P("tm", "rows", None), P("tm", "rows", None)),
        check_vma=False,
    )
```
